128 devices in a mesh: dp: 4 (over z), section: 4 (over y), expert: 8 (over x, core).
Axes of the slice: x: 4, y: 4, z: 4, core: 2. Of those that a mesh axis runs over, the one named last changes fastest.
Arguments:
- tokens: bfloat16 [4096, 5120], P(('dp', 'expert')), may hold values from -6 to 6
- cotangent: bfloat16 [4096, 5120], P(('dp', 'expert')), may hold values from -6 to 6
- norm_gain: float32 [4, 5120], P('section'), may hold values from 0.25 to 1.75
- route_gates: float32 [4, 4096, 6], P('section', ('dp', 'expert')), may hold values from 0.5 to 2
- expert_ids: int32 [4, 4096, 6], P('section', ('dp', 'expert')), may hold values from 0 to 159, as said below
- expert_map: int32 [4, 8], P('section'), may hold values from 0 to 7, each once within a row
- w_gate: bfloat16 [4, 8, 5120, 768], P('section', 'expert', 'dp'), may hold values from -0.078125 to 0.078125
- w_up: bfloat16 [4, 8, 5120, 768], P('section', 'expert', 'dp'), may hold values from -0.078125 to 0.078125
- w_down: bfloat16 [4, 8, 768, 5120], P('section', 'expert', None, 'dp'), may hold values from -0.21875 to 0.21875
Outputs:
- layer_out: bfloat16 [4, 4096, 5120], P('section', ('dp', 'expert'))
- input_grad: bfloat16 [4, 4096, 5120], P('section', ('dp', 'expert'))
- grad_gate: bfloat16 [4, 8, 5120, 768], P('section', 'expert', 'dp')
- grad_up: bfloat16 [4, 8, 5120, 768], P('section', 'expert', 'dp')
- grad_down: bfloat16 [4, 8, 768, 5120], P('section', 'expert', None, 'dp')
The draws below stay inside these ranges and needn't reach their ends.
Inputs may be any that keep to these rules, and one draw needn't show every extreme that they name: `expert_ids`: each token names 6 different experts on each layer. The held experts are those below 8. Split the 128 tokens of one index pair of dp and expert in order into 4 equal blocks: in each block each held expert is named by at most 2 tokens, and on every layer one held expert is named by exactly 2 tokens of every block, so by 8 tokens of every such pair. `expert_map`: each layer's row names every held expert once.
All inputs are finite; a program needn't handle non-finite values.
Results may differ from the reference program's by a relative error of at most 0.03.
Values may be sent and summed in bfloat16 or wider, within the bound.
No kernel may reach another device: no remote copies, remote signals or barrier semaphores. Data moves between devices by JAX's collectives and lax.ppermute only.
A program may use at most 128 MiB of HBM per device.

```python
import jax
import jax.numpy as jnp
from jax import lax

D = 5120
H = 768
NEXP = 160
TOPK = 6
MICRO = 4
CAP_MB = 2
TOK_DEV = 128
CAP = 8
SECTIONS = 4
E_WIN = 8
TOKENS = 4096
N_DP = 4
N_EXPERT = 8


def draw_expert_ids(key, part):
    span = TOK_DEV // MICRO
    blocks = TOKENS // span
    keys = jax.random.split(jax.random.fold_in(key, 11), 4)
    base = jax.random.randint(keys[0], (SECTIONS, TOKENS, NEXP), 0, 2 ** 20) * NEXP + jnp.arange(NEXP, dtype=jnp.int32)
    counts = jax.random.randint(keys[1], (SECTIONS, blocks, E_WIN), (CAP_MB + 1) // 2, CAP_MB + 1)
    fullest = jax.random.randint(keys[2], (SECTIONS, 1, 1), 0, E_WIN)
    column = jnp.arange(E_WIN, dtype=jnp.int32)
    is_full = column[None, None, :] == fullest
    counts = jnp.where(is_full, CAP_MB, counts)
    noise = jax.random.randint(keys[3], (SECTIONS, blocks, E_WIN, span), 0, 2 ** 20) * span + jnp.arange(span, dtype=jnp.int32)
    ranks = jnp.argsort(jnp.argsort(noise, axis=-1), axis=-1)
    chosen = ranks < counts[..., None]
    chosen = jnp.transpose(chosen, (0, 1, 3, 2)).reshape(SECTIONS, TOKENS, E_WIN)
    held_scores = jnp.where(chosen, jnp.where(is_full, 2 ** 29, 2 ** 28 + column[None, None, :]), -1 - column[None, None, :])
    scores = jnp.concatenate([held_scores.astype(jnp.int32), base[:, :, E_WIN:].astype(jnp.int32)], axis=2)
    return lax.top_k(scores, TOPK)[1].astype(jnp.int32)


def levels(key, extent, shards, smallest, high):
    loudness, own = 1.0, jax.random.fold_in(key, 6)
    for position, parts in shards:
        steps = jnp.exp(jax.random.uniform(jax.random.fold_in(own, position), (parts,), jnp.float32, smallest / len(shards), high / len(shards)))
        loudness = loudness * jnp.repeat(steps, extent[position] // parts).reshape([-1 if axis == position else 1 for axis in range(len(extent))])
    return loudness


def centred(stream_key, extent, scale, bound, cuts=(), held_as=jnp.bfloat16):
    entries = scale * jax.random.normal(stream_key, extent, jnp.float32)
    if cuts:
        entries = entries * levels(stream_key, extent, cuts, -0.22, 0.18)
    return jnp.clip(entries, -bound, bound).astype(held_as)


def setup_inputs(seed: int = 0) -> dict:
    streams_of = jax.random.split(jax.random.key(seed), 10)
    tokens = centred(streams_of[0], (TOKENS, D), 1.0, 6.0, ((0, 32),))
    cotangent = centred(streams_of[1], (TOKENS, D), 1.0, 6.0, ((0, 32),))
    norm_gain = jnp.clip(1.0 + 0.15 * jax.random.normal(streams_of[2], (SECTIONS, D), jnp.float32), 0.25, 1.75)
    route_gates = jnp.clip(0.5 + 1.5 * jax.random.uniform(streams_of[3], (SECTIONS, TOKENS, TOPK), jnp.float32) ** levels(streams_of[3], (SECTIONS, TOKENS, TOPK), ((0, 4), (1, 32)), -0.2, 0.2), 0.5, 2.0)
    expert_ids = draw_expert_ids(jax.random.fold_in(streams_of[9], 71), 0)
    expert_map = jax.vmap(lambda own: jax.random.permutation(own, E_WIN))(jax.random.split(streams_of[5], SECTIONS)).reshape((SECTIONS, E_WIN)).astype(jnp.int32)
    w_gate = centred(streams_of[6], (SECTIONS, E_WIN, D, H), D ** -0.5, 0.078125, ((0, 4), (1, 8), (2, 4)))
    w_up = centred(streams_of[7], (SECTIONS, E_WIN, D, H), D ** -0.5, 0.078125, ((0, 4), (1, 8), (2, 4)))
    w_down = centred(streams_of[8], (SECTIONS, E_WIN, H, D), H ** -0.5, 0.21875, ((0, 4), (1, 8), (3, 4)))
    return {"tokens": tokens, "cotangent": cotangent, "norm_gain": norm_gain, "route_gates": route_gates, "expert_ids": expert_ids, "expert_map": expert_map, "w_gate": w_gate, "w_up": w_up, "w_down": w_down}


def reference(tokens, cotangent, norm_gain, route_gates, expert_ids, expert_map, w_gate, w_up, w_down):
    slot_total = N_DP * N_EXPERT * CAP
    current = tokens
    outputs = []
    records = []
    for layer in range(SECTIONS):
        wide_in = current.astype(jnp.float32)
        inv_rms = lax.rsqrt(lax.optimization_barrier(jnp.mean(wide_in * wide_in, axis=1, keepdims=True)) + 1e-06)
        normed = (wide_in * inv_rms * norm_gain[layer][None, :]).astype(jnp.bfloat16)
        combined = jnp.zeros((TOKENS, D), jnp.float32)
        details = []
        for column in range(E_WIN):
            expert = expert_map[layer, column]
            matches = expert_ids[layer] == expert
            chosen = jnp.any(matches, axis=1)
            weight_row = lax.optimization_barrier(jnp.sum(jnp.where(matches, route_gates[layer], jnp.float32(0.0)), axis=1))
            picked = jnp.nonzero(chosen, size=slot_total, fill_value=TOKENS)[0].astype(jnp.int32)
            slot_rows = jnp.take(normed, picked, axis=0, mode='fill', fill_value=0)
            slot_weight = jnp.take(weight_row, picked, axis=0, mode='fill', fill_value=0)
            gate_pre = jnp.dot(slot_rows, w_gate[layer, column], preferred_element_type=jnp.float32)
            up_pre = jnp.dot(slot_rows, w_up[layer, column], preferred_element_type=jnp.float32)
            activated = (gate_pre * jax.nn.sigmoid(gate_pre) * up_pre).astype(jnp.bfloat16)
            expert_out = jnp.dot(activated, w_down[layer, column], preferred_element_type=jnp.float32).astype(jnp.bfloat16)
            combined = combined.at[picked].add(slot_weight[:, None] * expert_out.astype(jnp.float32), mode='drop')
            details.append((picked, slot_rows, slot_weight, gate_pre, up_pre, activated))
        result = (wide_in + combined).astype(jnp.bfloat16)
        outputs.append(result)
        records.append((wide_in, inv_rms, details))
        current = result
    incoming = cotangent
    input_grads = [None] * SECTIONS
    gate_grads = [None] * SECTIONS
    up_grads = [None] * SECTIONS
    down_grads = [None] * SECTIONS
    for layer in range(SECTIONS - 1, -1, -1):
        wide_in, inv_rms, details = records[layer]
        grad_wide = incoming.astype(jnp.float32)
        normed_grad = jnp.zeros((TOKENS, D), jnp.float32)
        layer_gate = []
        layer_up = []
        layer_down = []
        for column in range(E_WIN):
            picked, slot_rows, slot_weight, gate_pre, up_pre, activated = details[column]
            slot_grad = (slot_weight[:, None] * jnp.take(grad_wide, picked, axis=0, mode='fill', fill_value=0)).astype(jnp.bfloat16)
            layer_down.append(jnp.dot(activated.T, slot_grad, preferred_element_type=jnp.float32).astype(jnp.bfloat16))
            hidden_grad = jnp.dot(slot_grad, w_down[layer, column].T, preferred_element_type=jnp.float32)
            sigma = jax.nn.sigmoid(gate_pre)
            gate_grad = (hidden_grad * up_pre * sigma * (1.0 + gate_pre * (1.0 - sigma))).astype(jnp.bfloat16)
            up_grad = (hidden_grad * gate_pre * sigma).astype(jnp.bfloat16)
            layer_gate.append(jnp.dot(slot_rows.T, gate_grad, preferred_element_type=jnp.float32).astype(jnp.bfloat16))
            layer_up.append(jnp.dot(slot_rows.T, up_grad, preferred_element_type=jnp.float32).astype(jnp.bfloat16))
            slot_back = (jnp.dot(gate_grad, w_gate[layer, column].T, preferred_element_type=jnp.float32) + jnp.dot(up_grad, w_up[layer, column].T, preferred_element_type=jnp.float32)).astype(jnp.bfloat16)
            normed_grad = normed_grad.at[picked].add(slot_back.astype(jnp.float32), mode='drop')
        scaled_grad = normed_grad * norm_gain[layer][None, :]
        through_norm = inv_rms * (scaled_grad - wide_in * inv_rms * inv_rms * lax.optimization_barrier(jnp.mean(scaled_grad * wide_in, axis=1, keepdims=True)))
        incoming = (grad_wide + through_norm).astype(jnp.bfloat16)
        input_grads[layer] = incoming
        gate_grads[layer] = jnp.stack(layer_gate)
        up_grads[layer] = jnp.stack(layer_up)
        down_grads[layer] = jnp.stack(layer_down)
    return (jnp.stack(outputs), jnp.stack(input_grads), jnp.stack(gate_grads), jnp.stack(up_grads), jnp.stack(down_grads))
```

```python
import jax
import jax.numpy as jnp
from jax import lax
from jax.experimental import pallas as pl
from jax.experimental.pallas import tpu as pltpu
from jax.sharding import PartitionSpec as P

CAP = 8
EPS = 1e-06
BF = jnp.bfloat16
F32 = jnp.float32


def ring(value, axis, steps):
    count = lax.axis_size(axis)
    return lax.ppermute(value, axis, [(i, (i + steps) % count) for i in range(count)])


def hop(value, steps):
    count = lax.axis_size("section")
    pairs = [(i, i + steps) for i in range(count) if 0 <= i + steps < count]
    return lax.ppermute(value, "section", pairs)


def hop_back(value, steps, k):
    sections, experts = lax.axis_size("section"), lax.axis_size("expert")
    pairs = [
        (s * experts + e, (s + steps) * experts + (e - k) % experts)
        for s in range(sections)
        if 0 <= s + steps < sections
        for e in range(experts)
    ]
    return lax.ppermute(value, ("section", "expert"), pairs)


def mm(a, b, ca=1, cb=0):
    return lax.dot_general(a, b, (((ca,), (cb,)), ((), ())), preferred_element_type=F32)


def split(x):
    hi = lax.reduce_precision(x, 8, 7)
    mid = lax.reduce_precision(x - hi, 8, 7)
    low = x - hi - mid
    return [hi.astype(BF), mid.astype(BF), low.astype(BF)]


def from_lanes(x, at):
    return sum(x[:, at + i : at + i + 1].astype(F32) for i in range(3))


TILE = 256


def nt(a, b):
    return lax.dot_general(a, b, (((1,), (1,)), ((), ())), preferred_element_type=F32)


def tiles(extent):
    return [(i, min(TILE, extent - i)) for i in range(0, extent, TILE)]


def lane_pack(x):
    hi = x.astype(BF).astype(F32)
    mid = (x - hi).astype(BF).astype(F32)
    low = x - hi - mid
    lane = lax.broadcasted_iota(jnp.int32, (x.shape[0], 128), 1)
    return jnp.where(lane == 0, hi, jnp.where(lane == 1, mid, jnp.where(lane == 2, low, 0.0)))


def lane_sum(x):
    lane = lax.broadcasted_iota(jnp.int32, x.shape, 1)
    return jnp.sum(jnp.where(lane < 3, x.astype(F32), 0.0), axis=1, keepdims=True)


def regroup(refs, at, size, groups):
    loaded = [ref[:, at : at + size].astype(F32) for ref in refs]
    return [jnp.concatenate([x[j * CAP : (j + 1) * CAP] for x in loaded], axis=0) for j in range(groups)]


def put_blocks(value, refs, at, size, groups):
    experts = len(refs)
    own = experts * CAP
    for k, ref in enumerate(refs):
        rows = [value[j * own + k * CAP : j * own + (k + 1) * CAP] for j in range(groups)]
        ref[:, at : at + size] = jnp.concatenate(rows, axis=0).astype(BF)


def call(kernel, ins, outs, scratch=(), flops=0):
    moved = sum(x.size * x.dtype.itemsize for x in ins) + sum(o.size * o.dtype.itemsize for o in outs)
    return pl.pallas_call(
        kernel,
        out_shape=tuple(outs),
        in_specs=[pl.BlockSpec(memory_space=pltpu.VMEM)] * len(ins),
        out_specs=tuple(pl.BlockSpec(memory_space=pltpu.VMEM) for _ in outs),
        scratch_shapes=list(scratch),
        cost_estimate=pl.CostEstimate(flops=flops, bytes_accessed=moved, transcendentals=0),
    )(*ins)


def shape(dtype, *dims):
    return jax.ShapeDtypeStruct(dims, dtype)


def owner(state, back, tables, send_table, scale, experts):
    count, width = state.shape
    slots = send_table.shape[0]
    block = slots // experts

    def kernel(*refs):
        state_ref, refs = refs[0], refs[1:]
        back_refs, refs = refs[: len(back)], refs[len(back) :]
        table_refs, refs = refs[: len(tables)], refs[len(tables) :]
        send_ref, refs = refs[0], refs[1:]
        if scale is not None:
            scale_ref, refs = refs[0], refs[1:]
        new_ref, out_refs = refs[0], refs[1:]
        for at, size in tiles(width):
            rows = jnp.concatenate([ref[:, at : at + size] for ref in back_refs], axis=0)
            total = state_ref[:, at : at + size].astype(F32)
            for table_ref in table_refs:
                total = total + mm(table_ref[...], rows)
            new = total.astype(BF)
            new_ref[:, at : at + size] = new
            picked = mm(send_ref[...], new)
            if scale is not None:
                picked = picked * scale_ref[...]
            picked = picked.astype(BF)
            for k in range(experts):
                out_refs[k][:, at : at + size] = picked[k * block : (k + 1) * block]

    ins = [state, *back, *tables, send_table] + ([] if scale is None else [scale])
    outs = [shape(BF, count, width)] + [shape(BF, block, width)] * experts
    res = call(kernel, ins, outs, flops=2 * count * slots * width * (1 + len(tables)))
    return res[0], res[1:]


def forward_in(blocks, gain, gate_w, up_w, groups):
    experts = len(blocks)
    block, width = blocks[0].shape
    own, slots = experts * CAP, experts * block
    hidden = gate_w.shape[1]

    def kernel(*refs):
        block_refs, refs = refs[:experts], refs[experts:]
        gain_ref, gate_ref, up_ref, slot_ref, own_ref = refs[:5]
        part_refs, scaled_ref = refs[5:-1], refs[-1]
        squares = [jnp.zeros((own, 1), F32) for _ in range(groups)]
        for at, size in tiles(width):
            for j, x in enumerate(regroup(block_refs, at, size, groups)):
                slot_ref[j * own : (j + 1) * own, at : at + size] = x.astype(BF)
                scaled_ref[j * own : (j + 1) * own, at : at + size] = (x * gain_ref[:, at : at + size]).astype(BF)
                squares[j] = squares[j] + jnp.sum(x * x, axis=1, keepdims=True)
        for base, w_ref in ((0, gate_ref), (hidden, up_ref)):
            for at, size in tiles(hidden):
                part = mm(scaled_ref[...], w_ref[:, at : at + size])
                own_ref[:, base + at : base + at + size] = part[:own]
                for j in range(1, groups):
                    part_refs[j - 1][:, base + at : base + at + size] = part[j * own : (j + 1) * own].astype(BF)
        own_ref[:, 2 * hidden :] = lane_pack(squares[0])
        for j in range(1, groups):
            part_refs[j - 1][:, 2 * hidden :] = lane_pack(squares[j]).astype(BF)

    outs = [shape(BF, slots, width), shape(F32, own, 2 * hidden + 128)]
    outs += [shape(BF, own, 2 * hidden + 128)] * (groups - 1)
    res = call(
        kernel,
        [*blocks, gain, gate_w, up_w],
        outs,
        [pltpu.VMEM((slots, width), BF)],
        flops=4 * slots * width * hidden,
    )
    return res[0], res[1], res[2:]


def forward_act(first, parts, model):
    own, span = first.shape
    hidden = (span - 128) // 2

    def kernel(*refs):
        first_ref = refs[0]
        part_refs = refs[1 : 1 + len(parts)]
        pay_ref, gate_ref, up_ref = refs[1 + len(parts) :]
        square = lane_sum(first_ref[:, 2 * hidden :])
        for ref in part_refs:
            square = square + lane_sum(ref[:, 2 * hidden :])
        inv = lax.rsqrt(square / model + EPS)
        for at, size in tiles(hidden):
            gate = first_ref[:, at : at + size]
            up = first_ref[:, hidden + at : hidden + at + size]
            for ref in part_refs:
                gate = gate + ref[:, at : at + size].astype(F32)
                up = up + ref[:, hidden + at : hidden + at + size].astype(F32)
            gate, up = inv * gate, inv * up
            gate_ref[:, at : at + size] = gate
            up_ref[:, at : at + size] = up
            pay_ref[:, at : at + size] = (gate * jax.nn.sigmoid(gate) * up).astype(BF)
        pay_ref[:, hidden:] = lane_pack(inv).astype(BF)

    outs = [shape(BF, own, hidden + 128), shape(F32, own, hidden), shape(F32, own, hidden)]
    return call(kernel, [first, *parts], outs)


def forward_out(gathered, down_w, experts):
    groups = len(gathered)
    own, span = gathered[0].shape
    hidden, width = down_w.shape
    slots = groups * own

    def kernel(*refs):
        gathered_refs, refs = refs[:groups], refs[groups:]
        down_ref, all_ref, out_ref = refs[:3]
        block_refs = refs[3:]
        for j, ref in enumerate(gathered_refs):
            all_ref[j * own : (j + 1) * own, :] = ref[...]
        for at, size in tiles(width):
            part = mm(all_ref[:, :hidden], down_ref[:, at : at + size])
            out_ref[:, at : at + size] = part.astype(BF)
            put_blocks(part, block_refs, at, size, groups)

    outs = [shape(BF, slots, span), shape(BF, slots, width)] + [shape(BF, groups * CAP, width)] * experts
    res = call(kernel, [*gathered, down_w], outs, flops=2 * slots * hidden * width)
    return res[0], res[1], res[2:]


def backward_in(blocks, down_w, groups):
    experts = len(blocks)
    block, width = blocks[0].shape
    own, slots = experts * CAP, experts * block
    hidden = down_w.shape[0]

    def kernel(*refs):
        block_refs, refs = refs[:experts], refs[experts:]
        down_ref, grad_ref, own_ref = refs[:3]
        part_refs = refs[3:]
        for at, size in tiles(width):
            for j, x in enumerate(regroup(block_refs, at, size, groups)):
                grad_ref[j * own : (j + 1) * own, at : at + size] = x.astype(BF)
        for at, size in tiles(hidden):
            part = nt(grad_ref[...], down_ref[at : at + size, :])
            own_ref[:, at : at + size] = part[:own]
            for j in range(1, groups):
                part_refs[j - 1][:, at : at + size] = part[j * own : (j + 1) * own].astype(BF)

    outs = [shape(BF, slots, width), shape(F32, own, hidden)] + [shape(BF, own, hidden)] * (groups - 1)
    res = call(kernel, [*blocks, down_w], outs, flops=2 * slots * width * hidden)
    return res[0], res[1], res[2:]


def backward_act(first, parts, gate_pre, up_pre):
    own, hidden = first.shape

    def kernel(*refs):
        first_ref = refs[0]
        part_refs = refs[1 : 1 + len(parts)]
        gate_ref, up_ref, pay_ref = refs[1 + len(parts) :]
        inner = jnp.zeros((own, 1), F32)
        for at, size in tiles(hidden):
            hid = first_ref[:, at : at + size]
            for ref in part_refs:
                hid = hid + ref[:, at : at + size].astype(F32)
            gate, up = gate_ref[:, at : at + size], up_ref[:, at : at + size]
            sig = jax.nn.sigmoid(gate)
            gate_grad = (hid * up * sig * (1.0 + gate * (1.0 - sig))).astype(BF)
            up_grad = (hid * gate * sig).astype(BF)
            pay_ref[:, at : at + size] = gate_grad
            pay_ref[:, hidden + at : hidden + at + size] = up_grad
            both = gate_grad.astype(F32) * gate + up_grad.astype(F32) * up
            inner = inner + jnp.sum(both, axis=1, keepdims=True)
        pay_ref[:, 2 * hidden :] = lane_pack(inner).astype(BF)

    outs = [shape(BF, own, 2 * hidden + 128)]
    return call(kernel, [first, *parts, gate_pre, up_pre], outs)[0]


def backward_out(gathered, kept, slot, gain, gate_w, up_w, experts, model):
    groups = len(gathered)
    own, span = gathered[0].shape
    width, hidden = gate_w.shape
    slots = groups * own

    def kernel(*refs):
        gathered_refs, refs = refs[:groups], refs[groups:]
        kept_ref, slot_ref, gain_ref, gate_ref, up_ref, all_ref, given_ref = refs[:7]
        block_refs = refs[7:]
        for j, ref in enumerate(gathered_refs):
            all_ref[j * own : (j + 1) * own, :] = ref[...]
        inv = lane_sum(kept_ref[:, hidden:])
        lean = lane_sum(all_ref[:, 2 * hidden :]) * inv * inv / model
        for at, size in tiles(width):
            part = nt(all_ref[:, :hidden], gate_ref[at : at + size, :])
            part = part + nt(all_ref[:, hidden : 2 * hidden], up_ref[at : at + size, :])
            given = inv * gain_ref[:, at : at + size] * part - slot_ref[:, at : at + size].astype(F32) * lean
            given_ref[:, at : at + size] = given.astype(BF)
            put_blocks(given, block_refs, at, size, groups)

    outs = [shape(BF, slots, span), shape(BF, slots, width)] + [shape(BF, groups * CAP, width)] * experts
    res = call(
        kernel, [*gathered, kept, slot, gain, gate_w, up_w], outs, flops=4 * slots * hidden * width
    )
    return res[0], res[1], res[2:]


def local(tokens, cotangent, norm_gain, route_gates, expert_ids, expert_map, w_gate, w_up, w_down):
    section = lax.axis_index("section")
    d = lax.axis_index("dp")
    me = lax.axis_index("expert")
    sections, groups, experts = lax.axis_size("section"), lax.axis_size("dp"), lax.axis_size("expert")
    gate_w, up_w, down_w = w_gate[0, 0], w_up[0, 0], w_down[0, 0]
    rows, model = tokens.shape
    width, hidden = gate_w.shape
    own = experts * CAP
    slots = groups * own
    block = groups * CAP
    gain = lax.dynamic_slice(norm_gain, (0, d * width), (1, width))

    matches = expert_ids[0][:, :, None] == expert_map[0][None, None, :]
    chosen = jnp.any(matches, axis=1)
    weight = jnp.sum(jnp.where(matches, route_gates[0][:, :, None], 0.0), axis=1)
    lower = lax.broadcasted_iota(jnp.int32, (rows, rows), 0) > lax.broadcasted_iota(jnp.int32, (rows, rows), 1)
    before = mm(lower.astype(BF), chosen.astype(BF))
    code = jnp.where(chosen, before, -1.0)
    turn = (
        lax.broadcasted_iota(jnp.int32, (experts, experts), 0)
        == (lax.broadcasted_iota(jnp.int32, (experts, experts), 1) + me) % experts
    )
    pick = lambda x: jnp.sum(jnp.where(turn[None], x[:, :, None], 0.0), axis=1)
    mine = jnp.concatenate([pick(code), pick(weight)], axis=1)
    all_groups = [mine] + [None] * (groups - 1)
    for j in range(1, groups):
        all_groups[groups - j] = ring(mine, "dp", j)
    here = jnp.concatenate(all_groups, axis=0)
    behind = hop(here, 1)
    ahead = hop(here, -1)

    def spread(table, per, count):
        total = table.shape[0]
        col = lax.broadcasted_iota(jnp.int32, (experts, count), 1)
        wide = (col // per == lax.broadcasted_iota(jnp.int32, (experts, count), 0)).astype(BF)
        codes = table[:, :experts].astype(BF)
        weights = split(table[:, experts:])
        slot_col = lax.broadcasted_iota(jnp.int32, (total, count), 1)
        tok_row = lax.broadcasted_iota(jnp.int32, (total, count), 0)
        hit_back = (mm(codes, wide) == (slot_col % CAP).astype(F32)) & ((slot_col // CAP) % (per // CAP) == tok_row // rows)
        slot_row = lax.broadcasted_iota(jnp.int32, (count, total), 0)
        tok_col = lax.broadcasted_iota(jnp.int32, (count, total), 1)
        hit_out = (mm(wide, codes, 0, 1) == (slot_row % CAP).astype(F32)) & ((slot_row // CAP) % (per // CAP) == tok_col // rows)

        def weighted():
            return [jnp.where(hit_back, mm(w, wide), 0.0).astype(BF) for w in weights[:2]]

        def slot_weight():
            full = sum(mm(wide, w, 0, 1) for w in weights)
            return jnp.sum(jnp.where(hit_out, full, 0.0), axis=1, keepdims=True)

        return hit_out, hit_back, weighted, slot_weight

    hit_out, hit_back, own_weighted, own_slot_weight = spread(mine, CAP, own)
    own_out, own_back = hit_out.astype(BF), hit_back.astype(BF)
    own_w = own_weighted()
    own_r = own_slot_weight()
    hit_out, _, _, here_slot_weight = spread(here, block, slots)
    send_table = hit_out.astype(BF)
    send_r = here_slot_weight()
    _, _, behind_weighted, _ = spread(behind, block, slots)
    behind_w = behind_weighted()
    _, hit_back, _, _ = spread(ahead, block, slots)
    ahead_t = hit_back.astype(BF)

    def cut(value, j):
        return lax.dynamic_slice_in_dim(value, ((d + j) % groups) * width, width, axis=1)

    def to_slices(value):
        out = [cut(value, 0)] + [None] * (groups - 1)
        for j in range(1, groups):
            out[groups - j] = ring(cut(value, j), "dp", j)
        return out

    def to_rows(parts):
        return [parts[0]] + [ring(parts[j], "dp", j) for j in range(1, groups)]

    def absolute(parts):
        stacked = jnp.stack(parts)
        return jnp.concatenate(
            [lax.dynamic_index_in_dim(stacked, (d - b) % groups, 0, keepdims=False) for b in range(groups)], axis=1
        )

    def by_expert(value):
        shaped = value.reshape(groups, experts, CAP, value.shape[-1])
        return [shaped[:, k].reshape(block, value.shape[-1]) for k in range(experts)]

    def to_experts(blocks):
        return [blocks[0]] + [ring(blocks[k], "expert", k) for k in range(1, experts)]

    def first_rows(value, scale):
        picked = mm(own_out, value)
        picked = picked.astype(BF) if scale is None else (scale * picked).astype(BF)
        return to_experts(by_expert(jnp.concatenate(to_slices(picked), axis=0)))

    def reduce_groups(parts):
        return [ring(part, "dp", j + 1) for j, part in enumerate(parts)]

    def gather_groups(value):
        out = [value] + [None] * (groups - 1)
        for j in range(1, groups):
            out[groups - j] = ring(value, "dp", j)
        return out

    def keep(at, latest, earlier):
        if earlier is None:
            return latest
        return jax.tree.map(lambda a, b: jnp.where(section == at, a, b), latest, earlier)

    def finish(state, moved, tables):
        base = to_rows([state[j * rows : (j + 1) * rows] for j in range(groups)])
        parts = jnp.concatenate(to_rows([moved[j * own : (j + 1) * own] for j in range(groups)]), axis=1)
        blocks = [parts[k * CAP : (k + 1) * CAP] for k in range(experts)]
        back = jnp.concatenate([blocks[0]] + [ring(blocks[k], "expert", -k) for k in range(1, experts)], axis=0)
        added = sum(mm(t, back) for t in tables)
        return absolute(
            [(base[j].astype(F32) + added[:, j * width : (j + 1) * width]).astype(BF) for j in range(groups)]
        )

    received = first_rows(tokens, None)
    state = jnp.concatenate(to_slices(tokens), axis=0)
    early = first_rows(cotangent, own_r)
    incoming = jnp.concatenate(to_slices(cotangent), axis=0)

    saved, base, back = None, None, None
    for step in range(sections):
        if step:
            state, picked = owner(base, back, behind_w, send_table, None, experts)
            received = to_experts(picked)
        if step + 1 < sections:
            base = state if step == 0 else hop(state, 1)
        slot, first, parts = forward_in(received, gain, gate_w, up_w, groups)
        parts = reduce_groups(parts)
        payload, gate_pre, up_pre = forward_act(first, parts, model)
        gathered = gather_groups(payload)
        kept, out, blocks = forward_out(gathered, down_w, experts)
        if step + 1 < sections:
            back = [hop_back(blocks[k], 1, k) for k in range(experts)]
        saved = keep(step, (slot, gate_pre, up_pre, kept, out, state), saved)

    slot, gate_pre, up_pre, kept, out, state = saved
    layer_result = finish(state, out, own_w)

    final = None
    base, state = incoming, incoming
    for step in range(sections):
        at = sections - 1 - step
        if step == 0:
            received = early
        else:
            state, picked = owner(base, back, [ahead_t], send_table, send_r, experts)
            received = to_experts(picked)
            if step + 1 < sections:
                base = hop(state, -1)
        grad, first, parts = backward_in(received, down_w, groups)
        parts = reduce_groups(parts)
        payload = backward_act(first, parts, gate_pre, up_pre)
        gathered = gather_groups(payload)
        grads, given, blocks = backward_out(gathered, kept, slot, gain, gate_w, up_w, experts, model)
        if step + 1 < sections:
            back = [hop_back(blocks[k], -1, k) for k in range(experts)]
        final = keep(at, (grad, grads, given, state), final)

    grad, grads, given, state = final
    grad_in = finish(state, given, [own_back])
    inv_all = from_lanes(kept, hidden)
    normed = (slot.astype(F32) * inv_all * gain).astype(BF)
    down_grad = mm(kept[:, :hidden], grad, 0, 0).astype(BF)
    gate_wgrad = mm(normed, grads[:, :hidden], 0, 0).astype(BF)
    up_wgrad = mm(normed, grads[:, hidden : 2 * hidden], 0, 0).astype(BF)
    return (
        layer_result[None],
        grad_in[None],
        gate_wgrad[None, None],
        up_wgrad[None, None],
        down_grad[None, None],
    )


def solution(mesh):
    return jax.shard_map(
        local,
        mesh=mesh,
        in_specs=(
            P(("dp", "expert"), None),
            P(("dp", "expert"), None),
            P("section", None),
            P("section", ("dp", "expert"), None),
            P("section", ("dp", "expert"), None),
            P("section", None),
            P("section", "expert", "dp", None),
            P("section", "expert", "dp", None),
            P("section", "expert", None, "dp"),
        ),
        out_specs=(
            P("section", ("dp", "expert"), None),
            P("section", ("dp", "expert"), None),
            P("section", "expert", "dp", None),
            P("section", "expert", "dp", None),
            P("section", "expert", None, "dp"),
        ),
        check_vma=False,
    )
```

```python
import jax
import jax.numpy as jnp
from jax import lax
from jax.experimental import pallas as pl
from jax.experimental.pallas import tpu as pltpu
from jax.sharding import PartitionSpec as P


CAP = 8
EPS = 1e-06
BF = jnp.bfloat16
F32 = jnp.float32


def ring(value, axis, steps):
    count = lax.axis_size(axis)
    return lax.ppermute(value, axis, [(i, (i + steps) % count) for i in range(count)])


def hop(value, steps):
    count = lax.axis_size("section")
    pairs = [(i, i + steps) for i in range(count) if 0 <= i + steps < count]
    return lax.ppermute(value, "section", pairs)


def hop_back(value, steps, k):
    sections, experts = lax.axis_size("section"), lax.axis_size("expert")
    pairs = [
        (s * experts + e, (s + steps) * experts + (e - k) % experts)
        for s in range(sections)
        if 0 <= s + steps < sections
        for e in range(experts)
    ]
    return lax.ppermute(value, ("section", "expert"), pairs)


def mm(a, b, ca=1, cb=0):
    return lax.dot_general(a, b, (((ca,), (cb,)), ((), ())), preferred_element_type=F32)


def split(x):
    hi = lax.reduce_precision(x, 8, 7)
    mid = lax.reduce_precision(x - hi, 8, 7)
    low = x - hi - mid
    return [hi.astype(BF), mid.astype(BF), low.astype(BF)]


def from_lanes(x, at):
    return sum(x[:, at + i : at + i + 1].astype(F32) for i in range(3))


TILE = 256


def nt(a, b):
    return lax.dot_general(a, b, (((1,), (1,)), ((), ())), preferred_element_type=F32)


def tiles(extent):
    return [(i, min(TILE, extent - i)) for i in range(0, extent, TILE)]


def lane_pack(x):
    hi = x.astype(BF).astype(F32)
    mid = (x - hi).astype(BF).astype(F32)
    low = x - hi - mid
    lane = lax.broadcasted_iota(jnp.int32, (x.shape[0], 128), 1)
    return jnp.where(lane == 0, hi, jnp.where(lane == 1, mid, jnp.where(lane == 2, low, 0.0)))


def lane_sum(x):
    lane = lax.broadcasted_iota(jnp.int32, x.shape, 1)
    return jnp.sum(jnp.where(lane < 3, x.astype(F32), 0.0), axis=1, keepdims=True)


def regroup(refs, at, size, groups):
    loaded = [ref[:, at : at + size].astype(F32) for ref in refs]
    return [jnp.concatenate([x[j * CAP : (j + 1) * CAP] for x in loaded], axis=0) for j in range(groups)]


def put_blocks(value, refs, at, size, groups):
    experts = len(refs)
    own = experts * CAP
    for k, ref in enumerate(refs):
        rows = [value[j * own + k * CAP : j * own + (k + 1) * CAP] for j in range(groups)]
        ref[:, at : at + size] = jnp.concatenate(rows, axis=0).astype(BF)


def call(kernel, ins, outs, scratch=(), flops=0):
    moved = sum(x.size * x.dtype.itemsize for x in ins) + sum(o.size * o.dtype.itemsize for o in outs)
    return pl.pallas_call(
        kernel,
        out_shape=tuple(outs),
        in_specs=[pl.BlockSpec(memory_space=pltpu.VMEM)] * len(ins),
        out_specs=tuple(pl.BlockSpec(memory_space=pltpu.VMEM) for _ in outs),
        scratch_shapes=list(scratch),
        cost_estimate=pl.CostEstimate(flops=flops, bytes_accessed=moved, transcendentals=0),
    )(*ins)


def shape(dtype, *dims):
    return jax.ShapeDtypeStruct(dims, dtype)


def owner(state, back, tables, send_table, scale, experts):
    count, width = state.shape
    slots = send_table.shape[0]
    block = slots // experts

    def kernel(*refs):
        state_ref, refs = refs[0], refs[1:]
        back_refs, refs = refs[: len(back)], refs[len(back) :]
        table_refs, refs = refs[: len(tables)], refs[len(tables) :]
        send_ref, refs = refs[0], refs[1:]
        if scale is not None:
            scale_ref, refs = refs[0], refs[1:]
        new_ref, out_refs = refs[0], refs[1:]
        for at, size in tiles(width):
            rows = jnp.concatenate([ref[:, at : at + size] for ref in back_refs], axis=0)
            total = state_ref[:, at : at + size].astype(F32)
            for table_ref in table_refs:
                total = total + mm(table_ref[...], rows)
            new = total.astype(BF)
            new_ref[:, at : at + size] = new
            picked = mm(send_ref[...], new)
            if scale is not None:
                picked = picked * scale_ref[...]
            picked = picked.astype(BF)
            for k in range(experts):
                out_refs[k][:, at : at + size] = picked[k * block : (k + 1) * block]

    ins = [state, *back, *tables, send_table] + ([] if scale is None else [scale])
    outs = [shape(BF, count, width)] + [shape(BF, block, width)] * experts
    res = call(kernel, ins, outs, flops=2 * count * slots * width * (1 + len(tables)))
    return res[0], res[1:]


def forward_in(blocks, gain, gate_w, up_w, groups):
    experts = len(blocks)
    block, width = blocks[0].shape
    own, slots = experts * CAP, experts * block
    hidden = gate_w.shape[1]

    def kernel(*refs):
        block_refs, refs = refs[:experts], refs[experts:]
        gain_ref, gate_ref, up_ref, slot_ref, own_ref = refs[:5]
        part_refs, scaled_ref = refs[5:-1], refs[-1]
        squares = [jnp.zeros((own, 1), F32) for _ in range(groups)]
        for at, size in tiles(width):
            for j, x in enumerate(regroup(block_refs, at, size, groups)):
                slot_ref[j * own : (j + 1) * own, at : at + size] = x.astype(BF)
                scaled_ref[j * own : (j + 1) * own, at : at + size] = (x * gain_ref[:, at : at + size]).astype(BF)
                squares[j] = squares[j] + jnp.sum(x * x, axis=1, keepdims=True)
        for base, w_ref in ((0, gate_ref), (hidden, up_ref)):
            for at, size in tiles(hidden):
                part = mm(scaled_ref[...], w_ref[:, at : at + size])
                own_ref[:, base + at : base + at + size] = part[:own]
                for j in range(1, groups):
                    part_refs[j - 1][:, base + at : base + at + size] = part[j * own : (j + 1) * own].astype(BF)
        own_ref[:, 2 * hidden :] = lane_pack(squares[0])
        for j in range(1, groups):
            part_refs[j - 1][:, 2 * hidden :] = lane_pack(squares[j]).astype(BF)

    outs = [shape(BF, slots, width), shape(F32, own, 2 * hidden + 128)]
    outs += [shape(BF, own, 2 * hidden + 128)] * (groups - 1)
    res = call(
        kernel,
        [*blocks, gain, gate_w, up_w],
        outs,
        [pltpu.VMEM((slots, width), BF)],
        flops=4 * slots * width * hidden,
    )
    return res[0], res[1], res[2:]


def forward_act(first, parts, model):
    own, span = first.shape
    hidden = (span - 128) // 2

    def kernel(*refs):
        first_ref = refs[0]
        part_refs = refs[1 : 1 + len(parts)]
        pay_ref, gate_ref, up_ref = refs[1 + len(parts) :]
        square = lane_sum(first_ref[:, 2 * hidden :])
        for ref in part_refs:
            square = square + lane_sum(ref[:, 2 * hidden :])
        inv = lax.rsqrt(square / model + EPS)
        for at, size in tiles(hidden):
            gate = first_ref[:, at : at + size]
            up = first_ref[:, hidden + at : hidden + at + size]
            for ref in part_refs:
                gate = gate + ref[:, at : at + size].astype(F32)
                up = up + ref[:, hidden + at : hidden + at + size].astype(F32)
            gate, up = inv * gate, inv * up
            gate_ref[:, at : at + size] = gate
            up_ref[:, at : at + size] = up
            pay_ref[:, at : at + size] = (gate * jax.nn.sigmoid(gate) * up).astype(BF)
        pay_ref[:, hidden:] = lane_pack(inv).astype(BF)

    outs = [shape(BF, own, hidden + 128), shape(F32, own, hidden), shape(F32, own, hidden)]
    return call(kernel, [first, *parts], outs)


def forward_out(gathered, down_w, experts):
    groups = len(gathered)
    own, span = gathered[0].shape[0], down_w.shape[0] + 128
    hidden, width = down_w.shape
    slots = groups * own

    def kernel(*refs):
        gathered_refs, refs = refs[:groups], refs[groups:]
        down_ref, all_ref, out_ref = refs[:3]
        block_refs = refs[3:]
        for j, ref in enumerate(gathered_refs):
            all_ref[j * own : (j + 1) * own, :] = ref[:, :span]
        for at, size in tiles(width):
            part = mm(all_ref[:, :hidden], down_ref[:, at : at + size])
            out_ref[:, at : at + size] = part.astype(BF)
            put_blocks(part, block_refs, at, size, groups)

    outs = [shape(BF, slots, span), shape(BF, slots, width)] + [shape(BF, groups * CAP, width)] * experts
    res = call(kernel, [*gathered, down_w], outs, flops=2 * slots * hidden * width)
    return res[0], res[1], res[2:]


def backward_in(blocks, down_w, groups):
    experts = len(blocks)
    block, width = blocks[0].shape
    own, slots = experts * CAP, experts * block
    hidden = down_w.shape[0]

    def kernel(*refs):
        block_refs, refs = refs[:experts], refs[experts:]
        down_ref, grad_ref, own_ref = refs[:3]
        part_refs = refs[3:]
        for at, size in tiles(width):
            for j, x in enumerate(regroup(block_refs, at, size, groups)):
                grad_ref[j * own : (j + 1) * own, at : at + size] = x.astype(BF)
        for at, size in tiles(hidden):
            part = nt(grad_ref[...], down_ref[at : at + size, :])
            own_ref[:, at : at + size] = part[:own]
            for j in range(1, groups):
                part_refs[j - 1][:, at : at + size] = part[j * own : (j + 1) * own].astype(BF)

    outs = [shape(BF, slots, width), shape(F32, own, hidden)] + [shape(BF, own, hidden)] * (groups - 1)
    res = call(kernel, [*blocks, down_w], outs, flops=2 * slots * width * hidden)
    return res[0], res[1], res[2:]


def backward_act(first, parts, gate_pre, up_pre, lead=None):
    own, hidden = first.shape
    skip = 0 if lead is None else lead.shape[1]

    def kernel(*refs):
        first_ref = refs[0]
        part_refs = refs[1 : 1 + len(parts)]
        gate_ref, up_ref, whole_ref = refs[1 + len(parts) : 4 + len(parts)] if lead is None else refs[2 + len(parts) :]
        if lead is not None:
            whole_ref[:, :skip] = refs[1 + len(parts)][...]
        pay_ref = whole_ref.at[:, skip:]
        inner = jnp.zeros((own, 1), F32)
        for at, size in tiles(hidden):
            hid = first_ref[:, at : at + size]
            for ref in part_refs:
                hid = hid + ref[:, at : at + size].astype(F32)
            gate, up = gate_ref[:, at : at + size], up_ref[:, at : at + size]
            sig = jax.nn.sigmoid(gate)
            gate_grad = (hid * up * sig * (1.0 + gate * (1.0 - sig))).astype(BF)
            up_grad = (hid * gate * sig).astype(BF)
            pay_ref[:, at : at + size] = gate_grad
            pay_ref[:, hidden + at : hidden + at + size] = up_grad
            both = gate_grad.astype(F32) * gate + up_grad.astype(F32) * up
            inner = inner + jnp.sum(both, axis=1, keepdims=True)
        pay_ref[:, 2 * hidden :] = lane_pack(inner).astype(BF)

    outs = [shape(BF, own, skip + 2 * hidden + 128)]
    return call(kernel, [first, *parts] + ([] if lead is None else [lead]) + [gate_pre, up_pre], outs)[0]


def backward_out(gathered, kept, slot, gain, gate_w, up_w, experts, model):
    groups = len(gathered)
    own = gathered[0].shape[0]
    width, hidden = gate_w.shape
    slots = groups * own
    span = 2 * hidden + 128
    skip = gathered[0].shape[1] - span

    def kernel(*refs):
        gathered_refs, refs = refs[:groups], refs[groups:]
        kept_ref, slot_ref, gain_ref, gate_ref, up_ref, all_ref, given_ref = refs[:7]
        block_refs = refs[7:]
        for j, ref in enumerate(gathered_refs):
            all_ref[j * own : (j + 1) * own, :] = ref[:, skip:]
        inv = lane_sum(kept_ref[:, hidden:])
        lean = lane_sum(all_ref[:, 2 * hidden :]) * inv * inv / model
        for at, size in tiles(width):
            part = nt(all_ref[:, :hidden], gate_ref[at : at + size, :])
            part = part + nt(all_ref[:, hidden : 2 * hidden], up_ref[at : at + size, :])
            given = inv * gain_ref[:, at : at + size] * part - slot_ref[:, at : at + size].astype(F32) * lean
            given_ref[:, at : at + size] = given.astype(BF)
            put_blocks(given, block_refs, at, size, groups)

    outs = [shape(BF, slots, span), shape(BF, slots, width)] + [shape(BF, groups * CAP, width)] * experts
    res = call(
        kernel, [*gathered, kept, slot, gain, gate_w, up_w], outs, flops=4 * slots * hidden * width
    )
    return res[0], res[1], res[2:]


def stack(tokens, cotangent, norm_gain, route_gates, expert_ids, expert_map, w_gate, w_up, w_down):
    section = lax.axis_index("section")
    d = lax.axis_index("dp")
    me = lax.axis_index("expert")
    sections, groups, experts = lax.axis_size("section"), lax.axis_size("dp"), lax.axis_size("expert")
    gate_w, up_w, down_w = w_gate[0, 0], w_up[0, 0], w_down[0, 0]
    rows, model = tokens.shape
    width, hidden = gate_w.shape
    own = experts * CAP
    slots = groups * own
    block = groups * CAP
    gain = lax.dynamic_slice(norm_gain, (0, d * width), (1, width))

    matches = expert_ids[0][:, :, None] == expert_map[0][None, None, :]
    chosen = jnp.any(matches, axis=1)
    weight = jnp.sum(jnp.where(matches, route_gates[0][:, :, None], 0.0), axis=1)
    lower = lax.broadcasted_iota(jnp.int32, (rows, rows), 0) > lax.broadcasted_iota(jnp.int32, (rows, rows), 1)
    before = mm(lower.astype(BF), chosen.astype(BF))
    code = jnp.where(chosen, before, -1.0)
    turn = (
        lax.broadcasted_iota(jnp.int32, (experts, experts), 0)
        == (lax.broadcasted_iota(jnp.int32, (experts, experts), 1) + me) % experts
    )
    pick = lambda x: jnp.sum(jnp.where(turn[None], x[:, :, None], 0.0), axis=1)
    mine = jnp.concatenate([pick(code), pick(weight)], axis=1)

    def spread(table, per, count, turned):
        total = table.shape[0]
        col = lax.broadcasted_iota(jnp.int32, (experts, count), 1)
        wide = (col // per == lax.broadcasted_iota(jnp.int32, (experts, count), 0)).astype(BF)
        codes = table[:, :experts].astype(BF)
        weights = split(table[:, experts:])
        slot_col = lax.broadcasted_iota(jnp.int32, (total, count), 1)
        tok_row = lax.broadcasted_iota(jnp.int32, (total, count), 0)
        hit_back = (mm(codes, wide) == (slot_col % CAP).astype(F32)) & (((slot_col // CAP) % (per // CAP) + turned) % (per // CAP) == tok_row // rows)
        slot_row = lax.broadcasted_iota(jnp.int32, (count, total), 0)
        tok_col = lax.broadcasted_iota(jnp.int32, (count, total), 1)
        hit_out = (mm(wide, codes, 0, 1) == (slot_row % CAP).astype(F32)) & (((slot_row // CAP) % (per // CAP) + turned) % (per // CAP) == tok_col // rows)

        def weighted():
            return [jnp.where(hit_back, mm(w, wide), 0.0).astype(BF) for w in weights[:2]]

        def slot_weight():
            full = sum(mm(wide, w, 0, 1) for w in weights)
            return jnp.sum(jnp.where(hit_out, full, 0.0), axis=1, keepdims=True)

        return hit_out, hit_back, weighted, slot_weight

    hit_out, hit_back, own_weighted, own_slot_weight = spread(mine, CAP, own, 0)
    own_out, own_back = hit_out.astype(BF), hit_back.astype(BF)
    own_w = own_weighted()
    own_r = own_slot_weight()

    def after(value, gate):
        return lax.optimization_barrier((value, gate))[0]

    def narrow(value):
        return lax.all_to_all(value, "dp", split_axis=1, concat_axis=0, tiled=True)

    def broad(value):
        return lax.all_to_all(value, "dp", split_axis=0, concat_axis=1, tiled=True)

    def cut(value, j):
        return lax.dynamic_slice_in_dim(value, ((d + j) % groups) * width, width, axis=1)

    def to_slices(value):
        out = [cut(value, 0)] + [None] * (groups - 1)
        for j in range(1, groups):
            out[groups - j] = ring(cut(value, j), "dp", j)
        return out

    def to_rows(parts):
        return [parts[0]] + [ring(parts[j], "dp", j) for j in range(1, groups)]

    def absolute(parts):
        stacked = jnp.stack(parts)
        return jnp.concatenate(
            [lax.dynamic_index_in_dim(stacked, (d - b) % groups, 0, keepdims=False) for b in range(groups)], axis=1
        )

    def by_expert(value):
        shaped = value.reshape(groups, experts, CAP, value.shape[-1])
        return [shaped[:, k].reshape(block, value.shape[-1]) for k in range(experts)]

    def to_experts(blocks):
        return [blocks[0]] + [ring(blocks[k], "expert", k) for k in range(1, experts)]

    def first_cut(value, scale):
        picked = mm(own_out, value)
        return to_slices(picked.astype(BF) if scale is None else (scale * picked).astype(BF))

    def first_blocks(parts):
        return by_expert(jnp.concatenate(parts, axis=0))

    def reduce_groups(parts):
        return [ring(part, "dp", j + 1) for j, part in enumerate(parts)]

    def gather_groups(value):
        out = [value] + [None] * (groups - 1)
        for j in range(1, groups):
            out[groups - j] = ring(value, "dp", j)
        return out

    def keep(at, latest, earlier):
        if earlier is None:
            return latest
        return jax.tree.map(lambda a, b: jnp.where(section == at, a, b), latest, earlier)

    def own_parts(moved):
        return to_rows([moved[j * own : (j + 1) * own] for j in range(groups)])

    def own_rows(parts):
        whole = absolute(parts)
        blocks = [whole[k * CAP : (k + 1) * CAP] for k in range(experts)]
        return jnp.concatenate([blocks[0]] + [ring(blocks[k], "expert", -k) for k in range(1, experts)], axis=0)

    def finish(base, rows_back, tables):
        return (base.astype(F32) + sum(mm(t, rows_back) for t in tables)).astype(BF)

    start_parts = first_cut(tokens, None)
    received = to_experts(first_blocks(start_parts))
    codes = after(mine, start_parts)
    codes = [codes] + [ring(codes, "dp", j) for j in range(1, groups)]
    received, codes = lax.optimization_barrier((received, codes))
    stacked = jnp.stack(codes)
    here = jnp.concatenate(
        [lax.dynamic_index_in_dim(stacked, (d - b) % groups, 0, keepdims=False) for b in range(groups)], axis=0
    )
    behind, ahead = hop(here, 1), hop(here, -1)
    hit_out, _, _, here_slot_weight = spread(here, block, slots, d)
    send_table = hit_out.astype(BF)
    send_r = here_slot_weight()
    _, _, behind_weighted, _ = spread(behind, block, slots, d)
    behind_w = behind_weighted()
    _, hit_back, _, _ = spread(ahead, block, slots, d)
    ahead_t = hit_back.astype(BF)

    saved, base, back, fills = None, None, None, {}
    for step in range(sections):
        final_step = step + 1 == sections
        if step:
            state, picked = owner(base, back, behind_w, send_table, None, experts)
            received = to_experts(picked)
        if final_step:
            grad0, first0, parts0 = backward_in(after(fills["early"], picked), down_w, groups)
            parts0 = reduce_groups(parts0)
            received, parts0 = lax.optimization_barrier((received, parts0))
        elif step:
            base = hop(state, 1)
        if step == 2:
            received, fills["cut"] = lax.optimization_barrier((received, fills["cut"]))
        slot, first, parts = forward_in(received, gain, gate_w, up_w, groups)
        if step == 2:
            fills["early"] = to_experts(first_blocks(after(fills["cut"], parts)))
        parts = reduce_groups(parts)
        if step == 0:
            parts, behind, ahead = lax.optimization_barrier((parts, behind, ahead))
        payload, gate_pre, up_pre = forward_act(first, parts, model)
        if final_step:
            break
        gathered = gather_groups(payload)
        if step == 2:
            gathered, fills["early"] = lax.optimization_barrier((gathered, fills["early"]))
        kept, out, blocks = forward_out(gathered, down_w, experts)
        if step == 0:
            base = narrow(after(tokens, blocks))
            state = base
        if step == 1:
            fills["cut"] = first_cut(after(cotangent, blocks), own_r)
        if step == 2:
            incoming = narrow(after(cotangent, blocks))
        back = [hop_back(blocks[k], 1, k) for k in range(experts)]
        if step == 2:
            back, incoming = lax.optimization_barrier((back, incoming))
        saved = keep(step, (slot, gate_pre, up_pre, kept, out, state), saved)

    at = sections - 1
    slot, gate_pre, up_pre, fwd_state = keep(
        at, (slot, gate_pre, up_pre, state), (saved[0], saved[1], saved[2], saved[5])
    )
    final = None
    base, state = incoming, incoming
    for step in range(sections):
        at = sections - 1 - step
        if step == 0:
            grad = grad0
            payload = backward_act(first0, parts0, gate_pre, up_pre, payload)
        else:
            state, picked = owner(base, back, [ahead_t], send_table, send_r, experts)
            received = to_experts(picked)
            if step + 1 < sections:
                base = hop(state, -1)
            else:
                last = broad(jnp.where(section == at, state, final[-1]))
            if step == 2:
                received, fills["out"] = lax.optimization_barrier((received, fills["out"]))
            grad, first, parts = backward_in(received, down_w, groups)
            if step == 2:
                rows_back = own_rows(after(fills["out"], parts))
            parts = reduce_groups(parts)
            if step == 3:
                parts, last = lax.optimization_barrier((parts, last))
            payload = backward_act(first, parts, gate_pre, up_pre)
        gathered = gather_groups(payload)
        if step == 0:
            kept, out, _ = forward_out(gathered, down_w, experts)
            kept, fwd_out = keep(at, (kept, out), saved[3:5])
        if step == 2:
            gathered, rows_back = lax.optimization_barrier((gathered, rows_back))
        grads, given, blocks = backward_out(gathered, kept, slot, gain, gate_w, up_w, experts, model)
        if step + 1 < sections:
            if step == 0:
                fills["base"] = broad(after(fwd_state, blocks))
            if step == 1:
                fills["out"] = own_parts(after(fwd_out, blocks))
            back = [hop_back(blocks[k], -1, k) for k in range(experts)]
            if step == 0:
                back, fills["base"] = lax.optimization_barrier((back, fills["base"]))
        final = keep(at, (grad, grads, given, state), final)

    layer_result = finish(fills["base"], rows_back, own_w)
    grad, grads, given, state = final
    grad_in = finish(last, own_rows(own_parts(given)), [own_back])
    inv_all = from_lanes(kept, hidden)
    normed = (slot.astype(F32) * inv_all * gain).astype(BF)
    down_grad = mm(kept[:, :hidden], grad, 0, 0).astype(BF)
    gate_wgrad = mm(normed, grads[:, :hidden], 0, 0).astype(BF)
    up_wgrad = mm(normed, grads[:, hidden : 2 * hidden], 0, 0).astype(BF)
    return (
        layer_result[None],
        grad_in[None],
        gate_wgrad[None, None],
        up_wgrad[None, None],
        down_grad[None, None],
    )


def solution(mesh):
    return jax.shard_map(
        stack,
        mesh=mesh,
        in_specs=(
            P(("dp", "expert"), None),
            P(("dp", "expert"), None),
            P("section", None),
            P("section", ("dp", "expert"), None),
            P("section", ("dp", "expert"), None),
            P("section", None),
            P("section", "expert", "dp", None),
            P("section", "expert", "dp", None),
            P("section", "expert", None, "dp"),
        ),
        out_specs=(
            P("section", ("dp", "expert"), None),
            P("section", ("dp", "expert"), None),
            P("section", "expert", "dp", None),
            P("section", "expert", "dp", None),
            P("section", "expert", None, "dp"),
        ),
        check_vma=False,
    )
```

```python
import math

import jax
import jax.numpy as jnp
from jax import lax
from jax.experimental import pallas as pl
from jax.experimental.pallas import tpu as pltpu
from jax.sharding import PartitionSpec as P


CAP = 8
EPS = 1e-06
BF = jnp.bfloat16
F32 = jnp.float32


def ring(value, axis, steps):
    count = lax.axis_size(axis)
    return lax.ppermute(value, axis, [(i, (i + steps) % count) for i in range(count)])


def ring_in(value, axis, steps, where):
    count = lax.axis_size(axis)
    sections = lax.axis_size("section")
    if axis == "dp":
        at = lambda s, i: (i % count) * sections + s
        axes = (axis, "section")
    else:
        at = lambda s, i: s * count + i % count
        axes = ("section", axis)
    return lax.ppermute(value, axes, [(at(s, i), at(s, i + steps)) for s in where for i in range(count)])


def hop(value, steps):
    count = lax.axis_size("section")
    pairs = [(i, i + steps) for i in range(count) if 0 <= i + steps < count]
    return lax.ppermute(value, "section", pairs)


def hop_back(value, steps, k):
    sections, experts = lax.axis_size("section"), lax.axis_size("expert")
    pairs = [
        (s * experts + e, (s + steps) * experts + (e - k) % experts)
        for s in range(sections)
        if 0 <= s + steps < sections
        for e in range(experts)
    ]
    return lax.ppermute(value, ("section", "expert"), pairs)


def mm(a, b, ca=1, cb=0):
    return lax.dot_general(a, b, (((ca,), (cb,)), ((), ())), preferred_element_type=F32)


def split(x):
    hi = lax.reduce_precision(x, 8, 7)
    mid = lax.reduce_precision(x - hi, 8, 7)
    low = x - hi - mid
    return [hi.astype(BF), mid.astype(BF), low.astype(BF)]


def from_lanes(x, at):
    return sum(x[:, at + i : at + i + 1].astype(F32) for i in range(3))


TILE = 256


def nt(a, b):
    return lax.dot_general(a, b, (((1,), (1,)), ((), ())), preferred_element_type=F32)


def tiles(extent):
    return [(i, min(TILE, extent - i)) for i in range(0, extent, TILE)]


def lane_pack(x):
    hi = x.astype(BF).astype(F32)
    mid = (x - hi).astype(BF).astype(F32)
    low = x - hi - mid
    lane = lax.broadcasted_iota(jnp.int32, (x.shape[0], 128), 1)
    return jnp.where(lane == 0, hi, jnp.where(lane == 1, mid, jnp.where(lane == 2, low, 0.0)))


def lane_sum(x):
    lane = lax.broadcasted_iota(jnp.int32, x.shape, 1)
    return jnp.sum(jnp.where(lane < 3, x.astype(F32), 0.0), axis=1, keepdims=True)


def regroup(refs, at, size, groups):
    loaded = [ref[:, at : at + size].astype(F32) for ref in refs]
    return [jnp.concatenate([x[j * CAP : (j + 1) * CAP] for x in loaded], axis=0) for j in range(groups)]


def put_blocks(value, refs, at, size, groups):
    experts = len(refs)
    own = experts * CAP
    for k, ref in enumerate(refs):
        rows = [value[j * own + k * CAP : j * own + (k + 1) * CAP] for j in range(groups)]
        ref[:, at : at + size] = jnp.concatenate(rows, axis=0).astype(BF)


def near(x):
    return pltpu.with_memory_space_constraint(x, pltpu.VMEM)


def call(kernel, ins, outs, scratch=(), flops=0):
    moved = sum(math.prod(x.shape) * jnp.dtype(x.dtype).itemsize for x in [*ins, *outs])
    return pl.pallas_call(
        kernel,
        out_shape=tuple(outs),
        in_specs=[pl.BlockSpec(memory_space=pltpu.VMEM)] * len(ins),
        out_specs=tuple(pl.BlockSpec(memory_space=pltpu.VMEM) for _ in outs),
        scratch_shapes=list(scratch),
        compiler_params=pltpu.CompilerParams(vmem_limit_bytes=16 << 20),
        cost_estimate=pl.CostEstimate(flops=flops, bytes_accessed=moved, transcendentals=0),
    )(*ins)


def fast(dtype, *dims):
    return pltpu.VMEM(dims, dtype)


def shape(dtype, *dims):
    return jax.ShapeDtypeStruct(dims, dtype)


def owner(state, back, tables, send_table, scale, experts):
    count, width = state.shape
    slots = send_table.shape[0]
    block = slots // experts

    def kernel(*refs):
        state_ref, refs = refs[0], refs[1:]
        back_refs, refs = refs[: len(back)], refs[len(back) :]
        table_refs, refs = refs[: len(tables)], refs[len(tables) :]
        send_ref, refs = refs[0], refs[1:]
        if scale is not None:
            scale_ref, refs = refs[0], refs[1:]
        new_ref, out_refs = refs[0], refs[1:]
        for at, size in tiles(width):
            rows = jnp.concatenate([ref[:, at : at + size] for ref in back_refs], axis=0)
            total = state_ref[:, at : at + size].astype(F32)
            for table_ref in table_refs:
                total = total + mm(table_ref[...], rows)
            new = total.astype(BF)
            new_ref[:, at : at + size] = new
            picked = mm(send_ref[...], new)
            if scale is not None:
                picked = picked * scale_ref[...]
            picked = picked.astype(BF)
            for k in range(experts):
                out_refs[k][:, at : at + size] = picked[k * block : (k + 1) * block]

    ins = [state, *map(near, back), *tables, send_table] + ([] if scale is None else [scale])
    outs = [shape(BF, count, width)] + [fast(BF, block, width)] * experts
    res = call(kernel, ins, outs, flops=2 * count * slots * width * (1 + len(tables)))
    return res[0], res[1:]


def forward_in(blocks, gain, gate_w, up_w, groups):
    experts = len(blocks)
    block, width = blocks[0].shape
    own, slots = experts * CAP, experts * block
    hidden = gate_w.shape[1]

    def kernel(*refs):
        block_refs, refs = refs[:experts], refs[experts:]
        gain_ref, gate_ref, up_ref, slot_ref, own_ref = refs[:5]
        part_refs, scaled_ref = refs[5:-1], refs[-1]
        squares = [jnp.zeros((own, 1), F32) for _ in range(groups)]
        for at, size in tiles(width):
            for j, x in enumerate(regroup(block_refs, at, size, groups)):
                slot_ref[j * own : (j + 1) * own, at : at + size] = x.astype(BF)
                scaled_ref[j * own : (j + 1) * own, at : at + size] = (x * gain_ref[:, at : at + size]).astype(BF)
                squares[j] = squares[j] + jnp.sum(x * x, axis=1, keepdims=True)
        for base, w_ref in ((0, gate_ref), (hidden, up_ref)):
            for at, size in tiles(hidden):
                part = mm(scaled_ref[...], w_ref[:, at : at + size])
                own_ref[:, base + at : base + at + size] = part[:own]
                for j in range(1, groups):
                    part_refs[j - 1][:, base + at : base + at + size] = part[j * own : (j + 1) * own].astype(BF)
        own_ref[:, 2 * hidden :] = lane_pack(squares[0])
        for j in range(1, groups):
            part_refs[j - 1][:, 2 * hidden :] = lane_pack(squares[j]).astype(BF)

    outs = [shape(BF, slots, width), fast(F32, own, 2 * hidden + 128)]
    outs += [fast(BF, own, 2 * hidden + 128)] * (groups - 1)
    res = call(
        kernel,
        [*map(near, blocks), gain, gate_w, up_w],
        outs,
        [pltpu.VMEM((slots, width), BF)],
        flops=4 * slots * width * hidden,
    )
    return res[0], res[1], res[2:]


def forward_act(first, parts, model):
    own, span = first.shape
    hidden = (span - 128) // 2

    def kernel(*refs):
        first_ref = refs[0]
        part_refs = refs[1 : 1 + len(parts)]
        pay_ref, gate_ref, up_ref = refs[1 + len(parts) :]
        square = lane_sum(first_ref[:, 2 * hidden :])
        for ref in part_refs:
            square = square + lane_sum(ref[:, 2 * hidden :])
        inv = lax.rsqrt(square / model + EPS)
        for at, size in tiles(hidden):
            gate = first_ref[:, at : at + size]
            up = first_ref[:, hidden + at : hidden + at + size]
            for ref in part_refs:
                gate = gate + ref[:, at : at + size].astype(F32)
                up = up + ref[:, hidden + at : hidden + at + size].astype(F32)
            gate, up = inv * gate, inv * up
            gate_ref[:, at : at + size] = gate
            up_ref[:, at : at + size] = up
            pay_ref[:, at : at + size] = (gate * jax.nn.sigmoid(gate) * up).astype(BF)
        pay_ref[:, hidden:] = lane_pack(inv).astype(BF)

    outs = [fast(BF, own, hidden + 128), shape(F32, own, hidden), shape(F32, own, hidden)]
    return call(kernel, [near(first), *map(near, parts)], outs)


def forward_out(gathered, down_w, experts):
    groups = len(gathered)
    own, span = gathered[0].shape[0], down_w.shape[0] + 128
    hidden, width = down_w.shape
    slots = groups * own

    def kernel(*refs):
        gathered_refs, refs = refs[:groups], refs[groups:]
        down_ref, all_ref, out_ref = refs[:3]
        block_refs = refs[3:]
        for j, ref in enumerate(gathered_refs):
            all_ref[j * own : (j + 1) * own, :] = ref[:, :span]
        for at, size in tiles(width):
            part = mm(all_ref[:, :hidden], down_ref[:, at : at + size])
            out_ref[:, at : at + size] = part.astype(BF)
            put_blocks(part, block_refs, at, size, groups)

    outs = [shape(BF, slots, span), shape(BF, slots, width)] + [fast(BF, groups * CAP, width)] * experts
    res = call(kernel, [*map(near, gathered), down_w], outs, flops=2 * slots * hidden * width)
    return res[0], res[1], res[2:]


def backward_in(blocks, down_w, groups):
    experts = len(blocks)
    block, width = blocks[0].shape
    own, slots = experts * CAP, experts * block
    hidden = down_w.shape[0]

    def kernel(*refs):
        block_refs, refs = refs[:experts], refs[experts:]
        down_ref, grad_ref, own_ref = refs[:3]
        part_refs = refs[3:]
        for at, size in tiles(width):
            for j, x in enumerate(regroup(block_refs, at, size, groups)):
                grad_ref[j * own : (j + 1) * own, at : at + size] = x.astype(BF)
        for at, size in tiles(hidden):
            part = nt(grad_ref[...], down_ref[at : at + size, :])
            own_ref[:, at : at + size] = part[:own]
            for j in range(1, groups):
                part_refs[j - 1][:, at : at + size] = part[j * own : (j + 1) * own].astype(BF)

    outs = [shape(BF, slots, width), fast(F32, own, hidden)] + [fast(BF, own, hidden)] * (groups - 1)
    res = call(kernel, [*map(near, blocks), down_w], outs, flops=2 * slots * width * hidden)
    return res[0], res[1], res[2:]


def backward_act(first, parts, gate_pre, up_pre, lead=None):
    own, hidden = first.shape
    skip = 0 if lead is None else lead.shape[1]

    def kernel(*refs):
        first_ref = refs[0]
        part_refs = refs[1 : 1 + len(parts)]
        gate_ref, up_ref, whole_ref = refs[1 + len(parts) : 4 + len(parts)] if lead is None else refs[2 + len(parts) :]
        if lead is not None:
            whole_ref[:, :skip] = refs[1 + len(parts)][...]
        pay_ref = whole_ref.at[:, skip:]
        inner = jnp.zeros((own, 1), F32)
        for at, size in tiles(hidden):
            hid = first_ref[:, at : at + size]
            for ref in part_refs:
                hid = hid + ref[:, at : at + size].astype(F32)
            gate, up = gate_ref[:, at : at + size], up_ref[:, at : at + size]
            sig = jax.nn.sigmoid(gate)
            gate_grad = (hid * up * sig * (1.0 + gate * (1.0 - sig))).astype(BF)
            up_grad = (hid * gate * sig).astype(BF)
            pay_ref[:, at : at + size] = gate_grad
            pay_ref[:, hidden + at : hidden + at + size] = up_grad
            both = gate_grad.astype(F32) * gate + up_grad.astype(F32) * up
            inner = inner + jnp.sum(both, axis=1, keepdims=True)
        pay_ref[:, 2 * hidden :] = lane_pack(inner).astype(BF)

    outs = [fast(BF, own, skip + 2 * hidden + 128)]
    return call(kernel, [near(first), *map(near, parts)] + ([] if lead is None else [near(lead)]) + [gate_pre, up_pre], outs)[0]


def backward_out(gathered, kept, slot, gain, gate_w, up_w, experts, model):
    groups = len(gathered)
    own = gathered[0].shape[0]
    width, hidden = gate_w.shape
    slots = groups * own
    span = 2 * hidden + 128
    skip = gathered[0].shape[1] - span

    def kernel(*refs):
        gathered_refs, refs = refs[:groups], refs[groups:]
        kept_ref, slot_ref, gain_ref, gate_ref, up_ref, all_ref, given_ref = refs[:7]
        block_refs = refs[7:]
        for j, ref in enumerate(gathered_refs):
            all_ref[j * own : (j + 1) * own, :] = ref[:, skip:]
        inv = lane_sum(kept_ref[:, hidden:])
        lean = lane_sum(all_ref[:, 2 * hidden :]) * inv * inv / model
        for at, size in tiles(width):
            part = nt(all_ref[:, :hidden], gate_ref[at : at + size, :])
            part = part + nt(all_ref[:, hidden : 2 * hidden], up_ref[at : at + size, :])
            given = inv * gain_ref[:, at : at + size] * part - slot_ref[:, at : at + size].astype(F32) * lean
            given_ref[:, at : at + size] = given.astype(BF)
            put_blocks(given, block_refs, at, size, groups)

    outs = [shape(BF, slots, span), shape(BF, slots, width)] + [fast(BF, groups * CAP, width)] * experts
    res = call(
        kernel, [*map(near, gathered), kept, slot, gain, gate_w, up_w], outs, flops=4 * slots * hidden * width
    )
    return res[0], res[1], res[2:]


def stack(tokens, cotangent, norm_gain, route_gates, expert_ids, expert_map, w_gate, w_up, w_down):
    section = lax.axis_index("section")
    d = lax.axis_index("dp")
    me = lax.axis_index("expert")
    sections, groups, experts = lax.axis_size("section"), lax.axis_size("dp"), lax.axis_size("expert")
    gate_w, up_w, down_w = w_gate[0, 0], w_up[0, 0], w_down[0, 0]
    rows, model = tokens.shape
    width, hidden = gate_w.shape
    own = experts * CAP
    slots = groups * own
    block = groups * CAP
    gain = lax.dynamic_slice(norm_gain, (0, d * width), (1, width))

    matches = expert_ids[0][:, :, None] == expert_map[0][None, None, :]
    chosen = jnp.any(matches, axis=1)
    weight = jnp.sum(jnp.where(matches, route_gates[0][:, :, None], 0.0), axis=1)
    lower = lax.broadcasted_iota(jnp.int32, (rows, rows), 0) > lax.broadcasted_iota(jnp.int32, (rows, rows), 1)
    before = mm(lower.astype(BF), chosen.astype(BF))
    code = jnp.where(chosen, before, -1.0)
    turn = (
        lax.broadcasted_iota(jnp.int32, (experts, experts), 0)
        == (lax.broadcasted_iota(jnp.int32, (experts, experts), 1) + me) % experts
    )
    pick = lambda x: jnp.sum(jnp.where(turn[None], x[:, :, None], 0.0), axis=1)
    mine = jnp.concatenate([pick(code), pick(weight)], axis=1)

    def spread(table, per, count, turned):
        total = table.shape[0]
        col = lax.broadcasted_iota(jnp.int32, (experts, count), 1)
        wide = (col // per == lax.broadcasted_iota(jnp.int32, (experts, count), 0)).astype(BF)
        codes = table[:, :experts].astype(BF)
        weights = split(table[:, experts:])
        slot_col = lax.broadcasted_iota(jnp.int32, (total, count), 1)
        tok_row = lax.broadcasted_iota(jnp.int32, (total, count), 0)
        hit_back = (mm(codes, wide) == (slot_col % CAP).astype(F32)) & (((slot_col // CAP) % (per // CAP) + turned) % (per // CAP) == tok_row // rows)
        slot_row = lax.broadcasted_iota(jnp.int32, (count, total), 0)
        tok_col = lax.broadcasted_iota(jnp.int32, (count, total), 1)
        hit_out = (mm(wide, codes, 0, 1) == (slot_row % CAP).astype(F32)) & (((slot_row // CAP) % (per // CAP) + turned) % (per // CAP) == tok_col // rows)

        def weighted():
            return [jnp.where(hit_back, mm(w, wide), 0.0).astype(BF) for w in weights[:2]]

        def slot_weight():
            full = sum(mm(wide, w, 0, 1) for w in weights)
            return jnp.sum(jnp.where(hit_out, full, 0.0), axis=1, keepdims=True)

        return hit_out, hit_back, weighted, slot_weight

    hit_out, hit_back, own_weighted, own_slot_weight = spread(mine, CAP, own, 0)
    own_out, own_back = hit_out.astype(BF), hit_back.astype(BF)
    own_w = own_weighted()
    own_r = own_slot_weight()

    def after(value, gate):
        return lax.optimization_barrier((value, gate))[0]

    def cut(value, j):
        return lax.dynamic_slice_in_dim(value, ((d + j) % groups) * width, width, axis=1)

    def to_slices(value):
        out = [cut(value, 0)] + [None] * (groups - 1)
        for j in range(1, groups):
            out[groups - j] = ring(cut(value, j), "dp", j)
        return out

    def narrow(value, where):
        out = [cut(value, 0)] + [None] * (groups - 1)
        for j in range(1, groups):
            out[groups - j] = ring_in(cut(value, j), "dp", j, where)
        return out

    def to_rows(parts):
        return [parts[0]] + [ring(parts[j], "dp", j) for j in range(1, groups)]

    def absolute(parts):
        stacked = jnp.stack(parts)
        return jnp.concatenate(
            [lax.dynamic_index_in_dim(stacked, (d - b) % groups, 0, keepdims=False) for b in range(groups)], axis=1
        )

    def by_expert(value):
        shaped = value.reshape(groups, experts, CAP, value.shape[-1])
        return [shaped[:, k].reshape(block, value.shape[-1]) for k in range(experts)]

    def to_experts(blocks, where=None):
        if where is None:
            return [blocks[0]] + [ring(blocks[k], "expert", k) for k in range(1, experts)]
        return [blocks[0]] + [ring_in(blocks[k], "expert", k, where) for k in range(1, experts)]

    def first_cut(value, scale):
        picked = mm(own_out, value)
        if scale is None:
            return to_slices(picked.astype(BF))
        return narrow((scale * picked).astype(BF), (sections - 1,))

    def first_blocks(parts):
        return by_expert(jnp.concatenate(parts, axis=0))

    def reduce_groups(parts):
        return [ring(part, "dp", j + 1) for j, part in enumerate(parts)]

    def gather_groups(value):
        out = [value] + [None] * (groups - 1)
        for j in range(1, groups):
            out[groups - j] = ring(value, "dp", j)
        return out

    def keep(at, latest, earlier):
        if earlier is None:
            return latest
        return jax.tree.map(lambda a, b: jnp.where(section == at, a, b), latest, earlier)

    def own_parts(moved):
        return to_rows([moved[j * own : (j + 1) * own] for j in range(groups)])

    def own_rows(parts):
        whole = absolute(parts)
        blocks = [whole[k * CAP : (k + 1) * CAP] for k in range(experts)]
        return jnp.concatenate([blocks[0]] + [ring(blocks[k], "expert", -k) for k in range(1, experts)], axis=0)

    def finish(base, rows_back, tables):
        return (base.astype(F32) + sum(mm(t, rows_back) for t in tables)).astype(BF)

    lower = tuple(range(sections - 1))
    start_parts = first_cut(tokens, None)
    received = to_experts(first_blocks(start_parts))
    codes = after(mine, start_parts)
    codes = [codes] + [ring(codes, "dp", j) for j in range(1, groups)]
    received, codes = lax.optimization_barrier((received, codes))
    here = jnp.concatenate([codes[(groups - j) % groups] for j in range(groups)], axis=0)
    begin = after(tokens, start_parts)
    begin = {j: ring_in(cut(begin, j), "dp", j, lower) for j in (1, 3)}
    hit_out, _, _, here_slot_weight = spread(here, block, slots, 0)
    send_table = hit_out.astype(BF)
    send_r = here_slot_weight()

    saved, back, fills = None, None, {}
    for step in range(sections):
        final_step = step + 1 == sections
        if step:
            state, picked = owner(base, back, behind_w, send_table, None, experts)
            received = to_experts(picked)
        if step and not final_step:
            base = hop(state, 1)
        slot, first, parts = forward_in(received, gain, gate_w, up_w, groups)
        if step == 1:
            fills["early"] = to_experts(first_blocks(after(fills["cut"], parts)))
        parts = reduce_groups(parts)
        payload, gate_pre, up_pre = forward_act(first, parts, model)
        if final_step:
            break
        gathered = gather_groups(payload)
        if step == 1:
            gathered, fills["early"] = lax.optimization_barrier((gathered, fills["early"]))
        if step == 0:
            codes = after(here, payload)
            behind, ahead = hop(codes, 1), hop(codes, -1)
            _, _, behind_weighted, _ = spread(behind, block, slots, 0)
            behind_w = behind_weighted()
            _, hit_back, _, _ = spread(ahead, block, slots, 0)
            ahead_t = hit_back.astype(BF)
            fills["cut"] = first_cut(after(cotangent, payload), own_r)
        kept, out, blocks = forward_out(gathered, down_w, experts)
        back = [hop_back(blocks[k], 1, k) for k in range(experts)]
        if step == 0:
            far = ring_in(cut(after(tokens, blocks), 2), "dp", 2, lower)
            base = jnp.concatenate([cut(tokens, 0), begin[groups - 1], far, begin[1]], axis=0)
            state = base
        if step == 1:
            incoming = jnp.concatenate(narrow(after(cotangent, blocks), lower), axis=0)
        if step == 2:
            grad0, first0, parts0 = backward_in(after(fills["early"], blocks), down_w, groups)
            parts0 = [ring_in(part, "dp", j + 1, (sections - 1,)) for j, part in enumerate(parts0)]
        saved = keep(step, (slot, gate_pre, up_pre, kept, out, state), saved)

    at = sections - 1
    slot, gate_pre, up_pre, fwd_state = keep(
        at, (slot, gate_pre, up_pre, state), (saved[0], saved[1], saved[2], saved[5])
    )
    final = None
    base, state = incoming, incoming
    for step in range(sections):
        at = sections - 1 - step
        if step == 0:
            grad = grad0
            payload = backward_act(first0, parts0, gate_pre, up_pre, payload)
        else:
            state, picked = owner(base, back, [ahead_t], send_table, send_r, experts)
            received = to_experts(picked)
            if step + 1 < sections:
                base = hop(state, -1)
            else:
                turn_back = jnp.where(section == at, state, final[-1])
                turn_back = [turn_back[j * rows : (j + 1) * rows] for j in range(groups)]
                near_parts = {j: ring_in(turn_back[j], "dp", j, lower) for j in (1, 3)}
            if step == 1:
                received, fills["base"] = lax.optimization_barrier((received, fills["base"]))
            if step == 2:
                received, fills["out"] = lax.optimization_barrier((received, fills["out"]))
            grad, first, parts = backward_in(received, down_w, groups)
            if step == 2:
                rows_back = own_rows(after(fills["out"], parts))
            parts = reduce_groups(parts)
            payload = backward_act(first, parts, gate_pre, up_pre)
        gathered = gather_groups(payload)
        if step == 0:
            kept, out, _ = forward_out(gathered, down_w, experts)
            kept, fwd_out = keep(at, (kept, out), saved[3:5])
        if step == 2:
            gathered, rows_back = lax.optimization_barrier((gathered, rows_back))
        grads, given, blocks = backward_out(gathered, kept, slot, gain, gate_w, up_w, experts, model)
        if step + 1 < sections:
            if step == 0:
                held = after(fwd_state, blocks)
                fills["base"] = to_rows([held[j * rows : (j + 1) * rows] for j in range(groups)])
            if step == 1:
                fills["out"] = own_parts(after(fwd_out, blocks))
            back = [hop_back(blocks[k], -1, k) for k in range(experts)]
        final = keep(at, (grad, grads, given, state), final)

    layer_base = jnp.where(section == 0, tokens, absolute(fills["base"]))
    layer_result = finish(layer_base, rows_back, own_w)
    grad, grads, given, state = final
    last_parts = own_parts(given)
    last_back = own_rows(last_parts)
    far_part = ring_in(after(turn_back[2], last_parts), "dp", 2, lower)
    last = absolute([turn_back[0], near_parts[1], far_part, near_parts[3]])
    last = jnp.where(section == sections - 1, cotangent, last)
    grad_in = finish(last, last_back, [own_back])
    inv_all = from_lanes(kept, hidden)
    normed = (slot.astype(F32) * inv_all * gain).astype(BF)
    down_grad = mm(kept[:, :hidden], grad, 0, 0).astype(BF)
    gate_wgrad = mm(normed, grads[:, :hidden], 0, 0).astype(BF)
    up_wgrad = mm(normed, grads[:, hidden : 2 * hidden], 0, 0).astype(BF)
    return (
        layer_result[None],
        grad_in[None],
        gate_wgrad[None, None],
        up_wgrad[None, None],
        down_grad[None, None],
    )


def solution(mesh):
    return jax.shard_map(
        stack,
        mesh=mesh,
        in_specs=(
            P(("dp", "expert"), None),
            P(("dp", "expert"), None),
            P("section", None),
            P("section", ("dp", "expert"), None),
            P("section", ("dp", "expert"), None),
            P("section", None),
            P("section", "expert", "dp", None),
            P("section", "expert", "dp", None),
            P("section", "expert", None, "dp"),
        ),
        out_specs=(
            P("section", ("dp", "expert"), None),
            P("section", ("dp", "expert"), None),
            P("section", "expert", "dp", None),
            P("section", "expert", "dp", None),
            P("section", "expert", None, "dp"),
        ),
        check_vma=False,
    )
```

```python
import math

import jax
import jax.numpy as jnp
from jax import lax
from jax.experimental import pallas as pl
from jax.experimental.pallas import tpu as pltpu
from jax.sharding import PartitionSpec as P


CAP = 8
EPS = 1e-06
BF = jnp.bfloat16
F32 = jnp.float32


def ring(value, axis, steps):
    count = lax.axis_size(axis)
    return lax.ppermute(value, axis, [(i, (i + steps) % count) for i in range(count)])


def ring_in(value, axis, steps, where):
    count = lax.axis_size(axis)
    sections = lax.axis_size("section")
    if axis == "dp":
        at = lambda s, i: (i % count) * sections + s
        axes = (axis, "section")
    else:
        at = lambda s, i: s * count + i % count
        axes = ("section", axis)
    return lax.ppermute(value, axes, [(at(s, i), at(s, i + steps)) for s in where for i in range(count)])


def hop(value, steps):
    count = lax.axis_size("section")
    pairs = [(i, i + steps) for i in range(count) if 0 <= i + steps < count]
    return lax.ppermute(value, "section", pairs)


def hop_back(value, steps, k):
    sections, experts = lax.axis_size("section"), lax.axis_size("expert")
    pairs = [
        (s * experts + e, (s + steps) * experts + (e - k) % experts)
        for s in range(sections)
        if 0 <= s + steps < sections
        for e in range(experts)
    ]
    return lax.ppermute(value, ("section", "expert"), pairs)


def mm(a, b, ca=1, cb=0):
    return lax.dot_general(a, b, (((ca,), (cb,)), ((), ())), preferred_element_type=F32)


def split(x):
    hi = lax.reduce_precision(x, 8, 7)
    mid = lax.reduce_precision(x - hi, 8, 7)
    low = x - hi - mid
    return [hi.astype(BF), mid.astype(BF), low.astype(BF)]


def from_lanes(x, at):
    return sum(x[:, at + i : at + i + 1].astype(F32) for i in range(3))


TILE = 256


def nt(a, b):
    return lax.dot_general(a, b, (((1,), (1,)), ((), ())), preferred_element_type=F32)


def tiles(extent):
    return [(i, min(TILE, extent - i)) for i in range(0, extent, TILE)]


def lane_pack(x):
    hi = x.astype(BF).astype(F32)
    mid = (x - hi).astype(BF).astype(F32)
    low = x - hi - mid
    lane = lax.broadcasted_iota(jnp.int32, (x.shape[0], 128), 1)
    return jnp.where(lane == 0, hi, jnp.where(lane == 1, mid, jnp.where(lane == 2, low, 0.0)))


def lane_sum(x):
    lane = lax.broadcasted_iota(jnp.int32, x.shape, 1)
    return jnp.sum(jnp.where(lane < 3, x.astype(F32), 0.0), axis=1, keepdims=True)


def regroup(refs, at, size, groups):
    loaded = [ref[:, at : at + size].astype(F32) for ref in refs]
    return [jnp.concatenate([x[j * CAP : (j + 1) * CAP] for x in loaded], axis=0) for j in range(groups)]


def put_blocks(value, refs, at, size, groups):
    experts = len(refs)
    own = experts * CAP
    for k, ref in enumerate(refs):
        rows = [value[j * own + k * CAP : j * own + (k + 1) * CAP] for j in range(groups)]
        ref[:, at : at + size] = jnp.concatenate(rows, axis=0).astype(BF)


def near(x):
    return pltpu.with_memory_space_constraint(x, pltpu.VMEM)


def call(kernel, ins, outs, scratch=(), flops=0):
    moved = sum(math.prod(x.shape) * jnp.dtype(x.dtype).itemsize for x in [*ins, *outs])
    return pl.pallas_call(
        kernel,
        out_shape=tuple(outs),
        in_specs=[pl.BlockSpec(memory_space=pltpu.VMEM)] * len(ins),
        out_specs=tuple(pl.BlockSpec(memory_space=pltpu.VMEM) for _ in outs),
        scratch_shapes=list(scratch),
        compiler_params=pltpu.CompilerParams(vmem_limit_bytes=16 << 20),
        cost_estimate=pl.CostEstimate(flops=flops, bytes_accessed=moved, transcendentals=0),
    )(*ins)


def fast(dtype, *dims):
    return pltpu.VMEM(dims, dtype)


def shape(dtype, *dims):
    return jax.ShapeDtypeStruct(dims, dtype)


def owner(state, back, tables, send_table, scale, experts):
    count, width = state.shape
    slots = send_table.shape[0]
    block = slots // experts

    def kernel(*refs):
        state_ref, refs = refs[0], refs[1:]
        back_refs, refs = refs[: len(back)], refs[len(back) :]
        table_refs, refs = refs[: len(tables)], refs[len(tables) :]
        send_ref, refs = refs[0], refs[1:]
        if scale is not None:
            scale_ref, refs = refs[0], refs[1:]
        new_ref, out_refs = refs[0], refs[1:]
        for at, size in tiles(width):
            rows = jnp.concatenate([ref[:, at : at + size] for ref in back_refs], axis=0)
            total = state_ref[:, at : at + size].astype(F32)
            for table_ref in table_refs:
                total = total + mm(table_ref[...], rows)
            new = total.astype(BF)
            new_ref[:, at : at + size] = new
            picked = mm(send_ref[...], new)
            if scale is not None:
                picked = picked * scale_ref[...]
            picked = picked.astype(BF)
            for k in range(experts):
                out_refs[k][:, at : at + size] = picked[k * block : (k + 1) * block]

    ins = [state, *map(near, back), *tables, send_table] + ([] if scale is None else [scale])
    outs = [shape(BF, count, width)] + [fast(BF, block, width)] * experts
    res = call(kernel, ins, outs, flops=2 * count * slots * width * (1 + len(tables)))
    return res[0], res[1:]


def forward_in(blocks, gain, gate_w, up_w, groups):
    experts = len(blocks)
    block, width = blocks[0].shape
    own, slots = experts * CAP, experts * block
    hidden = gate_w.shape[1]

    def kernel(*refs):
        block_refs, refs = refs[:experts], refs[experts:]
        gain_ref, gate_ref, up_ref, slot_ref, own_ref = refs[:5]
        part_refs, scaled_ref = refs[5:-1], refs[-1]
        squares = [jnp.zeros((own, 1), F32) for _ in range(groups)]
        for at, size in tiles(width):
            for j, x in enumerate(regroup(block_refs, at, size, groups)):
                slot_ref[j * own : (j + 1) * own, at : at + size] = x.astype(BF)
                scaled_ref[j * own : (j + 1) * own, at : at + size] = (x * gain_ref[:, at : at + size]).astype(BF)
                squares[j] = squares[j] + jnp.sum(x * x, axis=1, keepdims=True)
        for base, w_ref in ((0, gate_ref), (hidden, up_ref)):
            for at, size in tiles(hidden):
                part = mm(scaled_ref[...], w_ref[:, at : at + size])
                own_ref[:, base + at : base + at + size] = part[:own]
                for j in range(1, groups):
                    part_refs[j - 1][:, base + at : base + at + size] = part[j * own : (j + 1) * own].astype(BF)
        own_ref[:, 2 * hidden :] = lane_pack(squares[0])
        for j in range(1, groups):
            part_refs[j - 1][:, 2 * hidden :] = lane_pack(squares[j]).astype(BF)

    outs = [shape(BF, slots, width), fast(F32, own, 2 * hidden + 128)]
    outs += [fast(BF, own, 2 * hidden + 128)] * (groups - 1)
    res = call(
        kernel,
        [*map(near, blocks), gain, gate_w, up_w],
        outs,
        [pltpu.VMEM((slots, width), BF)],
        flops=4 * slots * width * hidden,
    )
    return res[0], res[1], res[2:]


def forward_act(first, parts, model):
    own, span = first.shape
    hidden = (span - 128) // 2

    def kernel(*refs):
        first_ref = refs[0]
        part_refs = refs[1 : 1 + len(parts)]
        pay_ref, gate_ref, up_ref = refs[1 + len(parts) :]
        square = lane_sum(first_ref[:, 2 * hidden :])
        for ref in part_refs:
            square = square + lane_sum(ref[:, 2 * hidden :])
        inv = lax.rsqrt(square / model + EPS)
        for at, size in tiles(hidden):
            gate = first_ref[:, at : at + size]
            up = first_ref[:, hidden + at : hidden + at + size]
            for ref in part_refs:
                gate = gate + ref[:, at : at + size].astype(F32)
                up = up + ref[:, hidden + at : hidden + at + size].astype(F32)
            gate, up = inv * gate, inv * up
            gate_ref[:, at : at + size] = gate
            up_ref[:, at : at + size] = up
            pay_ref[:, at : at + size] = (gate * jax.nn.sigmoid(gate) * up).astype(BF)
        pay_ref[:, hidden:] = lane_pack(inv).astype(BF)

    outs = [fast(BF, own, hidden + 128), shape(F32, own, hidden), shape(F32, own, hidden)]
    return call(kernel, [near(first), *map(near, parts)], outs)


def forward_out(gathered, down_w, experts):
    groups = len(gathered)
    own, span = gathered[0].shape[0], down_w.shape[0] + 128
    hidden, width = down_w.shape
    slots = groups * own

    def kernel(*refs):
        gathered_refs, refs = refs[:groups], refs[groups:]
        down_ref, all_ref, out_ref = refs[:3]
        block_refs = refs[3:]
        for j, ref in enumerate(gathered_refs):
            all_ref[j * own : (j + 1) * own, :] = ref[:, :span]
        for at, size in tiles(width):
            part = mm(all_ref[:, :hidden], down_ref[:, at : at + size])
            out_ref[:, at : at + size] = part.astype(BF)
            put_blocks(part, block_refs, at, size, groups)

    outs = [shape(BF, slots, span), shape(BF, slots, width)] + [fast(BF, groups * CAP, width)] * experts
    res = call(kernel, [*map(near, gathered), down_w], outs, flops=2 * slots * hidden * width)
    return res[0], res[1], res[2:]


def backward_in(blocks, down_w, groups):
    experts = len(blocks)
    block, width = blocks[0].shape
    own, slots = experts * CAP, experts * block
    hidden = down_w.shape[0]

    def kernel(*refs):
        block_refs, refs = refs[:experts], refs[experts:]
        down_ref, grad_ref, own_ref = refs[:3]
        part_refs = refs[3:]
        for at, size in tiles(width):
            for j, x in enumerate(regroup(block_refs, at, size, groups)):
                grad_ref[j * own : (j + 1) * own, at : at + size] = x.astype(BF)
        for at, size in tiles(hidden):
            part = nt(grad_ref[...], down_ref[at : at + size, :])
            own_ref[:, at : at + size] = part[:own]
            for j in range(1, groups):
                part_refs[j - 1][:, at : at + size] = part[j * own : (j + 1) * own].astype(BF)

    outs = [shape(BF, slots, width), fast(F32, own, hidden)] + [fast(BF, own, hidden)] * (groups - 1)
    res = call(kernel, [*map(near, blocks), down_w], outs, flops=2 * slots * width * hidden)
    return res[0], res[1], res[2:]


def backward_act(first, parts, gate_pre, up_pre, lead=None):
    own, hidden = first.shape
    skip = 0 if lead is None else lead.shape[1]

    def kernel(*refs):
        first_ref = refs[0]
        part_refs = refs[1 : 1 + len(parts)]
        gate_ref, up_ref, whole_ref = refs[1 + len(parts) : 4 + len(parts)] if lead is None else refs[2 + len(parts) :]
        if lead is not None:
            whole_ref[:, :skip] = refs[1 + len(parts)][...]
        pay_ref = whole_ref.at[:, skip:]
        inner = jnp.zeros((own, 1), F32)
        for at, size in tiles(hidden):
            hid = first_ref[:, at : at + size]
            for ref in part_refs:
                hid = hid + ref[:, at : at + size].astype(F32)
            gate, up = gate_ref[:, at : at + size], up_ref[:, at : at + size]
            sig = jax.nn.sigmoid(gate)
            gate_grad = (hid * up * sig * (1.0 + gate * (1.0 - sig))).astype(BF)
            up_grad = (hid * gate * sig).astype(BF)
            pay_ref[:, at : at + size] = gate_grad
            pay_ref[:, hidden + at : hidden + at + size] = up_grad
            both = gate_grad.astype(F32) * gate + up_grad.astype(F32) * up
            inner = inner + jnp.sum(both, axis=1, keepdims=True)
        pay_ref[:, 2 * hidden :] = lane_pack(inner).astype(BF)

    outs = [fast(BF, own, skip + 2 * hidden + 128)]
    return call(kernel, [near(first), *map(near, parts)] + ([] if lead is None else [near(lead)]) + [gate_pre, up_pre], outs)[0]


def backward_out(gathered, kept, slot, gain, gate_w, up_w, experts, model):
    groups = len(gathered)
    own = gathered[0].shape[0]
    width, hidden = gate_w.shape
    slots = groups * own
    span = 2 * hidden + 128
    skip = gathered[0].shape[1] - span

    def kernel(*refs):
        gathered_refs, refs = refs[:groups], refs[groups:]
        kept_ref, slot_ref, gain_ref, gate_ref, up_ref, all_ref, given_ref = refs[:7]
        block_refs = refs[7:]
        for j, ref in enumerate(gathered_refs):
            all_ref[j * own : (j + 1) * own, :] = ref[:, skip:]
        inv = lane_sum(kept_ref[:, hidden:])
        lean = lane_sum(all_ref[:, 2 * hidden :]) * inv * inv / model
        for at, size in tiles(width):
            part = nt(all_ref[:, :hidden], gate_ref[at : at + size, :])
            part = part + nt(all_ref[:, hidden : 2 * hidden], up_ref[at : at + size, :])
            given = inv * gain_ref[:, at : at + size] * part - slot_ref[:, at : at + size].astype(F32) * lean
            given_ref[:, at : at + size] = given.astype(BF)
            put_blocks(given, block_refs, at, size, groups)

    outs = [shape(BF, slots, span), shape(BF, slots, width)] + [fast(BF, groups * CAP, width)] * experts
    res = call(
        kernel, [*map(near, gathered), kept, slot, gain, gate_w, up_w], outs, flops=4 * slots * hidden * width
    )
    return res[0], res[1], res[2:]


def stack(tokens, cotangent, norm_gain, route_gates, expert_ids, expert_map, w_gate, w_up, w_down):
    section = lax.axis_index("section")
    d = lax.axis_index("dp")
    me = lax.axis_index("expert")
    sections, groups, experts = lax.axis_size("section"), lax.axis_size("dp"), lax.axis_size("expert")
    gate_w, up_w, down_w = w_gate[0, 0], w_up[0, 0], w_down[0, 0]
    rows, model = tokens.shape
    width, hidden = gate_w.shape
    own = experts * CAP
    slots = groups * own
    block = groups * CAP
    gain = lax.dynamic_slice(norm_gain, (0, d * width), (1, width))

    matches = expert_ids[0][:, :, None] == expert_map[0][None, None, :]
    chosen = jnp.any(matches, axis=1)
    weight = jnp.sum(jnp.where(matches, route_gates[0][:, :, None], 0.0), axis=1)
    lower = lax.broadcasted_iota(jnp.int32, (rows, rows), 0) > lax.broadcasted_iota(jnp.int32, (rows, rows), 1)
    before = mm(lower.astype(BF), chosen.astype(BF))
    code = jnp.where(chosen, before, -1.0)
    turn = (
        lax.broadcasted_iota(jnp.int32, (experts, experts), 0)
        == (lax.broadcasted_iota(jnp.int32, (experts, experts), 1) + me) % experts
    )
    pick = lambda x: jnp.sum(jnp.where(turn[None], x[:, :, None], 0.0), axis=1)
    mine = jnp.concatenate([pick(code), pick(weight)], axis=1)

    def spread(table, per, count, turned):
        total = table.shape[0]
        col = lax.broadcasted_iota(jnp.int32, (experts, count), 1)
        wide = (col // per == lax.broadcasted_iota(jnp.int32, (experts, count), 0)).astype(BF)
        codes = table[:, :experts].astype(BF)
        weights = split(table[:, experts:])
        slot_col = lax.broadcasted_iota(jnp.int32, (total, count), 1)
        tok_row = lax.broadcasted_iota(jnp.int32, (total, count), 0)
        hit_back = (mm(codes, wide) == (slot_col % CAP).astype(F32)) & (((slot_col // CAP) % (per // CAP) + turned) % (per // CAP) == tok_row // rows)
        slot_row = lax.broadcasted_iota(jnp.int32, (count, total), 0)
        tok_col = lax.broadcasted_iota(jnp.int32, (count, total), 1)
        hit_out = (mm(wide, codes, 0, 1) == (slot_row % CAP).astype(F32)) & (((slot_row // CAP) % (per // CAP) + turned) % (per // CAP) == tok_col // rows)

        def weighted():
            return [jnp.where(hit_back, mm(w, wide), 0.0).astype(BF) for w in weights[:2]]

        def slot_weight():
            full = sum(mm(wide, w, 0, 1) for w in weights)
            return jnp.sum(jnp.where(hit_out, full, 0.0), axis=1, keepdims=True)

        return hit_out, hit_back, weighted, slot_weight

    hit_out, hit_back, own_weighted, own_slot_weight = spread(mine, CAP, own, 0)
    own_out, own_back = hit_out.astype(BF), hit_back.astype(BF)
    own_w = own_weighted()
    own_r = own_slot_weight()

    def after(value, gate):
        return lax.optimization_barrier((value, gate))[0]

    def cut(value, j):
        return lax.dynamic_slice_in_dim(value, ((d + j) % groups) * width, width, axis=1)

    def to_slices(value):
        out = [cut(value, 0)] + [None] * (groups - 1)
        for j in range(1, groups):
            out[groups - j] = ring(cut(value, j), "dp", j)
        return out

    def narrow(value, where):
        out = [cut(value, 0)] + [None] * (groups - 1)
        for j in range(1, groups):
            out[groups - j] = ring_in(cut(value, j), "dp", j, where)
        return out

    def to_rows(parts):
        return [parts[0]] + [ring(parts[j], "dp", j) for j in range(1, groups)]

    def absolute(parts):
        stacked = jnp.stack(parts)
        return jnp.concatenate(
            [lax.dynamic_index_in_dim(stacked, (d - b) % groups, 0, keepdims=False) for b in range(groups)], axis=1
        )

    def by_expert(value):
        shaped = value.reshape(groups, experts, CAP, value.shape[-1])
        return [shaped[:, k].reshape(block, value.shape[-1]) for k in range(experts)]

    def to_experts(blocks, where=None):
        if where is None:
            return [blocks[0]] + [ring(blocks[k], "expert", k) for k in range(1, experts)]
        return [blocks[0]] + [ring_in(blocks[k], "expert", k, where) for k in range(1, experts)]

    def first_cut(value, scale):
        picked = mm(own_out, value)
        if scale is None:
            return to_slices(picked.astype(BF))
        return narrow((scale * picked).astype(BF), (sections - 1,))

    def first_blocks(parts):
        return by_expert(jnp.concatenate(parts, axis=0))

    def reduce_groups(parts):
        return [ring(part, "dp", j + 1) for j, part in enumerate(parts)]

    def gather_groups(value):
        out = [value] + [None] * (groups - 1)
        for j in range(1, groups):
            out[groups - j] = ring(value, "dp", j)
        return out

    def keep(at, latest, earlier):
        if earlier is None:
            return latest
        return jax.tree.map(lambda a, b: jnp.where(section == at, a, b), latest, earlier)

    def own_parts(moved):
        return to_rows([moved[j * own : (j + 1) * own] for j in range(groups)])

    def own_rows(parts):
        whole = absolute(parts)
        blocks = [whole[k * CAP : (k + 1) * CAP] for k in range(experts)]
        return jnp.concatenate([blocks[0]] + [ring(blocks[k], "expert", -k) for k in range(1, experts)], axis=0)

    def finish(base, rows_back, tables):
        return (base.astype(F32) + sum(mm(t, rows_back) for t in tables)).astype(BF)

    lower = tuple(range(sections - 1))
    start_parts = first_cut(tokens, None)
    received = to_experts(first_blocks(start_parts))
    codes = after(mine, start_parts)
    codes = [codes] + [ring(codes, "dp", j) for j in range(1, groups)]
    received, codes = lax.optimization_barrier((received, codes))
    here = jnp.concatenate([codes[(groups - j) % groups] for j in range(groups)], axis=0)
    begin = after(tokens, start_parts)
    begin = {j: ring_in(cut(begin, j), "dp", j, lower) for j in (1, 3)}
    hit_out, _, _, here_slot_weight = spread(here, block, slots, 0)
    send_table = hit_out.astype(BF)
    send_r = here_slot_weight()

    saved, back, fills = None, None, {}
    for step in range(sections):
        final_step = step + 1 == sections
        if step:
            state, picked = owner(base, back, behind_w, send_table, None, experts)
            received = to_experts(picked)
        if step and not final_step:
            base = hop(state, 1)
        slot, first, parts = forward_in(received, gain, gate_w, up_w, groups)
        if step == 1:
            fills["early"] = to_experts(first_blocks(after(fills["cut"], parts)))
        parts = reduce_groups(parts)
        payload, gate_pre, up_pre = forward_act(first, parts, model)
        if final_step:
            break
        gathered = gather_groups(payload)
        if step == 1:
            gathered, fills["early"] = lax.optimization_barrier((gathered, fills["early"]))
        if step == 0:
            codes = after(here, payload)
            behind, ahead = hop(codes, 1), hop(codes, -1)
            _, _, behind_weighted, _ = spread(behind, block, slots, 0)
            behind_w = behind_weighted()
            _, hit_back, _, _ = spread(ahead, block, slots, 0)
            ahead_t = hit_back.astype(BF)
            far = ring_in(cut(after(tokens, payload), 2), "dp", 2, lower)
            fills["cut"] = first_cut(after(cotangent, payload), own_r)
        kept, out, blocks = forward_out(gathered, down_w, experts)
        back = [hop_back(blocks[k], 1, k) for k in range(experts)]
        if step == 0:
            base = jnp.concatenate([cut(tokens, 0), begin[groups - 1], far, begin[1]], axis=0)
            state = base
        if step == 1:
            grad0, first0, parts0 = backward_in(after(fills["early"], blocks), down_w, groups)
            parts0 = [ring_in(part, "dp", j + 1, (sections - 1,)) for j, part in enumerate(parts0)]
        saved = keep(step, (slot, gate_pre, up_pre, kept, out, state), saved)

    at = sections - 1
    slot, gate_pre, up_pre, fwd_state = keep(
        at, (slot, gate_pre, up_pre, state), (saved[0], saved[1], saved[2], saved[5])
    )
    final, base = None, None
    for step in range(sections):
        at = sections - 1 - step
        if step == 0:
            grad = grad0
            payload = backward_act(first0, parts0, gate_pre, up_pre, payload)
            state = jnp.zeros_like(fwd_state)
        else:
            state, picked = owner(base, back, [ahead_t], send_table, send_r, experts)
            received = to_experts(picked)
            if step + 1 < sections:
                base = hop(state, -1)
            else:
                turn_back = jnp.where(section == at, state, final[-1])
                turn_back = [turn_back[j * rows : (j + 1) * rows] for j in range(groups)]
                near_parts = {j: ring_in(turn_back[j], "dp", j, lower) for j in (1, 3)}
            if step == 1:
                received, fills["base"] = lax.optimization_barrier((received, fills["base"]))
            if step == 2:
                received, fills["out"] = lax.optimization_barrier((received, fills["out"]))
            grad, first, parts = backward_in(received, down_w, groups)
            if step == 2:
                rows_back = own_rows(after(fills["out"], parts))
            parts = reduce_groups(parts)
            payload = backward_act(first, parts, gate_pre, up_pre)
        gathered = gather_groups(payload)
        if step == 0:
            base = jnp.concatenate(narrow(after(cotangent, payload), lower), axis=0)
            kept, out, _ = forward_out(gathered, down_w, experts)
            kept, fwd_out = keep(at, (kept, out), saved[3:5])
        if step == 2:
            gathered, rows_back = lax.optimization_barrier((gathered, rows_back))
        grads, given, blocks = backward_out(gathered, kept, slot, gain, gate_w, up_w, experts, model)
        if step + 1 < sections:
            if step == 0:
                held = after(fwd_state, blocks)
                fills["base"] = to_rows([held[j * rows : (j + 1) * rows] for j in range(groups)])
            if step == 1:
                fills["out"] = own_parts(after(fwd_out, blocks))
            back = [hop_back(blocks[k], -1, k) for k in range(experts)]
        final = keep(at, (grad, grads, given, state), final)

    layer_base = jnp.where(section == 0, tokens, absolute(fills["base"]))
    layer_result = finish(layer_base, rows_back, own_w)
    grad, grads, given, state = final
    last_parts = own_parts(given)
    last_back = own_rows(last_parts)
    far_part = ring_in(after(turn_back[2], last_parts), "dp", 2, lower)
    last = absolute([turn_back[0], near_parts[1], far_part, near_parts[3]])
    last = jnp.where(section == sections - 1, cotangent, last)
    grad_in = finish(last, last_back, [own_back])
    inv_all = from_lanes(kept, hidden)
    normed = (slot.astype(F32) * inv_all * gain).astype(BF)
    down_grad = mm(kept[:, :hidden], grad, 0, 0).astype(BF)
    gate_wgrad = mm(normed, grads[:, :hidden], 0, 0).astype(BF)
    up_wgrad = mm(normed, grads[:, hidden : 2 * hidden], 0, 0).astype(BF)
    return (
        layer_result[None],
        grad_in[None],
        gate_wgrad[None, None],
        up_wgrad[None, None],
        down_grad[None, None],
    )


def solution(mesh):
    return jax.shard_map(
        stack,
        mesh=mesh,
        in_specs=(
            P(("dp", "expert"), None),
            P(("dp", "expert"), None),
            P("section", None),
            P("section", ("dp", "expert"), None),
            P("section", ("dp", "expert"), None),
            P("section", None),
            P("section", "expert", "dp", None),
            P("section", "expert", "dp", None),
            P("section", "expert", None, "dp"),
        ),
        out_specs=(
            P("section", ("dp", "expert"), None),
            P("section", ("dp", "expert"), None),
            P("section", "expert", "dp", None),
            P("section", "expert", "dp", None),
            P("section", "expert", None, "dp"),
        ),
        check_vma=False,
    )
```

```python
import math

import jax
import jax.numpy as jnp
from jax import lax
from jax.experimental import pallas as pl
from jax.experimental.pallas import tpu as pltpu
from jax.sharding import PartitionSpec as P


CAP = 8
EPS = 1e-06
BF = jnp.bfloat16
F32 = jnp.float32


def ring(value, axis, steps):
    count = lax.axis_size(axis)
    return lax.ppermute(value, axis, [(i, (i + steps) % count) for i in range(count)])


def ring_in(value, axis, steps, where):
    count = lax.axis_size(axis)
    sections = lax.axis_size("section")
    if axis == "dp":
        at = lambda s, i: (i % count) * sections + s
        axes = (axis, "section")
    else:
        at = lambda s, i: s * count + i % count
        axes = ("section", axis)
    return lax.ppermute(value, axes, [(at(s, i), at(s, i + steps)) for s in where for i in range(count)])


def hop(value, steps):
    count = lax.axis_size("section")
    pairs = [(i, i + steps) for i in range(count) if 0 <= i + steps < count]
    return lax.ppermute(value, "section", pairs)


def hop_back(value, steps, k):
    sections, experts = lax.axis_size("section"), lax.axis_size("expert")
    pairs = [
        (s * experts + e, (s + steps) * experts + (e - k) % experts)
        for s in range(sections)
        if 0 <= s + steps < sections
        for e in range(experts)
    ]
    return lax.ppermute(value, ("section", "expert"), pairs)


def mm(a, b, ca=1, cb=0):
    return lax.dot_general(a, b, (((ca,), (cb,)), ((), ())), preferred_element_type=F32)


def split(x):
    hi = lax.reduce_precision(x, 8, 7)
    mid = lax.reduce_precision(x - hi, 8, 7)
    low = x - hi - mid
    return [hi.astype(BF), mid.astype(BF), low.astype(BF)]


def from_lanes(x, at):
    return sum(x[:, at + i : at + i + 1].astype(F32) for i in range(3))


TILE = 256


def nt(a, b):
    return lax.dot_general(a, b, (((1,), (1,)), ((), ())), preferred_element_type=F32)


def tiles(extent):
    return [(i, min(TILE, extent - i)) for i in range(0, extent, TILE)]


def lane_pack(x):
    hi = x.astype(BF).astype(F32)
    mid = (x - hi).astype(BF).astype(F32)
    low = x - hi - mid
    lane = lax.broadcasted_iota(jnp.int32, (x.shape[0], 128), 1)
    return jnp.where(lane == 0, hi, jnp.where(lane == 1, mid, jnp.where(lane == 2, low, 0.0)))


def lane_sum(x):
    lane = lax.broadcasted_iota(jnp.int32, x.shape, 1)
    return jnp.sum(jnp.where(lane < 3, x.astype(F32), 0.0), axis=1, keepdims=True)


def regroup(refs, at, size, groups):
    loaded = [ref[:, at : at + size].astype(F32) for ref in refs]
    return [jnp.concatenate([x[j * CAP : (j + 1) * CAP] for x in loaded], axis=0) for j in range(groups)]


def put_blocks(value, refs, at, size, groups):
    experts = len(refs)
    own = experts * CAP
    for k, ref in enumerate(refs):
        rows = [value[j * own + k * CAP : j * own + (k + 1) * CAP] for j in range(groups)]
        ref[:, at : at + size] = jnp.concatenate(rows, axis=0).astype(BF)


def near(x):
    return pltpu.with_memory_space_constraint(x, pltpu.VMEM)


def call(kernel, ins, outs, scratch=(), flops=0):
    moved = sum(math.prod(x.shape) * jnp.dtype(x.dtype).itemsize for x in [*ins, *outs])
    return pl.pallas_call(
        kernel,
        out_shape=tuple(outs),
        in_specs=[pl.BlockSpec(memory_space=pltpu.VMEM)] * len(ins),
        out_specs=tuple(pl.BlockSpec(memory_space=pltpu.VMEM) for _ in outs),
        scratch_shapes=list(scratch),
        compiler_params=pltpu.CompilerParams(vmem_limit_bytes=16 << 20),
        cost_estimate=pl.CostEstimate(flops=flops, bytes_accessed=moved, transcendentals=0),
    )(*ins)


def fast(dtype, *dims):
    return pltpu.VMEM(dims, dtype)


def shape(dtype, *dims):
    return jax.ShapeDtypeStruct(dims, dtype)


def owner(state, back, tables, send_table, scale, experts):
    count, width = state.shape
    slots = send_table.shape[0]
    block = slots // experts

    def kernel(*refs):
        state_ref, refs = refs[0], refs[1:]
        back_refs, refs = refs[: len(back)], refs[len(back) :]
        table_refs, refs = refs[: len(tables)], refs[len(tables) :]
        send_ref, refs = refs[0], refs[1:]
        if scale is not None:
            scale_ref, refs = refs[0], refs[1:]
        new_ref, out_refs = refs[0], refs[1:]
        for at, size in tiles(width):
            rows = jnp.concatenate([ref[:, at : at + size] for ref in back_refs], axis=0)
            total = state_ref[:, at : at + size].astype(F32)
            for table_ref in table_refs:
                total = total + mm(table_ref[...], rows)
            new = total.astype(BF)
            new_ref[:, at : at + size] = new
            picked = mm(send_ref[...], new)
            if scale is not None:
                picked = picked * scale_ref[...]
            picked = picked.astype(BF)
            for k in range(experts):
                out_refs[k][:, at : at + size] = picked[k * block : (k + 1) * block]

    ins = [state, *map(near, back), *tables, send_table] + ([] if scale is None else [scale])
    outs = [shape(BF, count, width)] + [fast(BF, block, width)] * experts
    res = call(kernel, ins, outs, flops=2 * count * slots * width * (1 + len(tables)))
    return res[0], res[1:]


def forward_in(blocks, gain, gate_w, up_w, groups):
    experts = len(blocks)
    block, width = blocks[0].shape
    own, slots = experts * CAP, experts * block
    hidden = gate_w.shape[1]

    def kernel(*refs):
        block_refs, refs = refs[:experts], refs[experts:]
        gain_ref, gate_ref, up_ref, slot_ref, own_ref = refs[:5]
        part_refs, scaled_ref = refs[5:-1], refs[-1]
        squares = [jnp.zeros((own, 1), F32) for _ in range(groups)]
        for at, size in tiles(width):
            for j, x in enumerate(regroup(block_refs, at, size, groups)):
                slot_ref[j * own : (j + 1) * own, at : at + size] = x.astype(BF)
                scaled_ref[j * own : (j + 1) * own, at : at + size] = (x * gain_ref[:, at : at + size]).astype(BF)
                squares[j] = squares[j] + jnp.sum(x * x, axis=1, keepdims=True)
        for base, w_ref in ((0, gate_ref), (hidden, up_ref)):
            for at, size in tiles(hidden):
                part = mm(scaled_ref[...], w_ref[:, at : at + size])
                own_ref[:, base + at : base + at + size] = part[:own]
                for j in range(1, groups):
                    part_refs[j - 1][:, base + at : base + at + size] = part[j * own : (j + 1) * own].astype(BF)
        own_ref[:, 2 * hidden :] = lane_pack(squares[0])
        for j in range(1, groups):
            part_refs[j - 1][:, 2 * hidden :] = lane_pack(squares[j]).astype(BF)

    outs = [shape(BF, slots, width), fast(F32, own, 2 * hidden + 128)]
    outs += [fast(BF, own, 2 * hidden + 128)] * (groups - 1)
    res = call(
        kernel,
        [*map(near, blocks), gain, gate_w, up_w],
        outs,
        [pltpu.VMEM((slots, width), BF)],
        flops=4 * slots * width * hidden,
    )
    return res[0], res[1], res[2:]


def forward_act(first, parts, model):
    own, span = first.shape
    hidden = (span - 128) // 2

    def kernel(*refs):
        first_ref = refs[0]
        part_refs = refs[1 : 1 + len(parts)]
        pay_ref, gate_ref, up_ref = refs[1 + len(parts) :]
        square = lane_sum(first_ref[:, 2 * hidden :])
        for ref in part_refs:
            square = square + lane_sum(ref[:, 2 * hidden :])
        inv = lax.rsqrt(square / model + EPS)
        for at, size in tiles(hidden):
            gate = first_ref[:, at : at + size]
            up = first_ref[:, hidden + at : hidden + at + size]
            for ref in part_refs:
                gate = gate + ref[:, at : at + size].astype(F32)
                up = up + ref[:, hidden + at : hidden + at + size].astype(F32)
            gate, up = inv * gate, inv * up
            gate_ref[:, at : at + size] = gate
            up_ref[:, at : at + size] = up
            pay_ref[:, at : at + size] = (gate * jax.nn.sigmoid(gate) * up).astype(BF)
        pay_ref[:, hidden:] = lane_pack(inv).astype(BF)

    outs = [fast(BF, own, hidden + 128), shape(F32, own, hidden), shape(F32, own, hidden)]
    return call(kernel, [near(first), *map(near, parts)], outs)


def forward_out(gathered, down_w, experts):
    groups = len(gathered)
    own, span = gathered[0].shape[0], down_w.shape[0] + 128
    hidden, width = down_w.shape
    slots = groups * own

    def kernel(*refs):
        gathered_refs, refs = refs[:groups], refs[groups:]
        down_ref, all_ref, out_ref = refs[:3]
        block_refs = refs[3:]
        for j, ref in enumerate(gathered_refs):
            all_ref[j * own : (j + 1) * own, :] = ref[:, :span]
        for at, size in tiles(width):
            part = mm(all_ref[:, :hidden], down_ref[:, at : at + size])
            out_ref[:, at : at + size] = part.astype(BF)
            put_blocks(part, block_refs, at, size, groups)

    outs = [shape(BF, slots, span), shape(BF, slots, width)] + [fast(BF, groups * CAP, width)] * experts
    res = call(kernel, [*map(near, gathered), down_w], outs, flops=2 * slots * hidden * width)
    return res[0], res[1], res[2:]


def backward_in(blocks, down_w, groups):
    experts = len(blocks)
    block, width = blocks[0].shape
    own, slots = experts * CAP, experts * block
    hidden = down_w.shape[0]

    def kernel(*refs):
        block_refs, refs = refs[:experts], refs[experts:]
        down_ref, grad_ref, own_ref = refs[:3]
        part_refs = refs[3:]
        for at, size in tiles(width):
            for j, x in enumerate(regroup(block_refs, at, size, groups)):
                grad_ref[j * own : (j + 1) * own, at : at + size] = x.astype(BF)
        for at, size in tiles(hidden):
            part = nt(grad_ref[...], down_ref[at : at + size, :])
            own_ref[:, at : at + size] = part[:own]
            for j in range(1, groups):
                part_refs[j - 1][:, at : at + size] = part[j * own : (j + 1) * own].astype(BF)

    outs = [shape(BF, slots, width), fast(F32, own, hidden)] + [fast(BF, own, hidden)] * (groups - 1)
    res = call(kernel, [*map(near, blocks), down_w], outs, flops=2 * slots * width * hidden)
    return res[0], res[1], res[2:]


def backward_act(first, parts, gate_pre, up_pre, lead=None):
    own, hidden = first.shape
    skip = 0 if lead is None else lead.shape[1]

    def kernel(*refs):
        first_ref = refs[0]
        part_refs = refs[1 : 1 + len(parts)]
        gate_ref, up_ref, whole_ref = refs[1 + len(parts) : 4 + len(parts)] if lead is None else refs[2 + len(parts) :]
        if lead is not None:
            whole_ref[:, :skip] = refs[1 + len(parts)][...]
        pay_ref = whole_ref.at[:, skip:]
        inner = jnp.zeros((own, 1), F32)
        for at, size in tiles(hidden):
            hid = first_ref[:, at : at + size]
            for ref in part_refs:
                hid = hid + ref[:, at : at + size].astype(F32)
            gate, up = gate_ref[:, at : at + size], up_ref[:, at : at + size]
            sig = jax.nn.sigmoid(gate)
            gate_grad = (hid * up * sig * (1.0 + gate * (1.0 - sig))).astype(BF)
            up_grad = (hid * gate * sig).astype(BF)
            pay_ref[:, at : at + size] = gate_grad
            pay_ref[:, hidden + at : hidden + at + size] = up_grad
            both = gate_grad.astype(F32) * gate + up_grad.astype(F32) * up
            inner = inner + jnp.sum(both, axis=1, keepdims=True)
        pay_ref[:, 2 * hidden :] = lane_pack(inner).astype(BF)

    outs = [fast(BF, own, skip + 2 * hidden + 128)]
    return call(kernel, [near(first), *map(near, parts)] + ([] if lead is None else [near(lead)]) + [gate_pre, up_pre], outs)[0]


def backward_out(gathered, kept, slot, gain, gate_w, up_w, experts, model):
    groups = len(gathered)
    own = gathered[0].shape[0]
    width, hidden = gate_w.shape
    slots = groups * own
    span = 2 * hidden + 128
    skip = gathered[0].shape[1] - span

    def kernel(*refs):
        gathered_refs, refs = refs[:groups], refs[groups:]
        kept_ref, slot_ref, gain_ref, gate_ref, up_ref, all_ref, given_ref = refs[:7]
        block_refs = refs[7:]
        for j, ref in enumerate(gathered_refs):
            all_ref[j * own : (j + 1) * own, :] = ref[:, skip:]
        inv = lane_sum(kept_ref[:, hidden:])
        lean = lane_sum(all_ref[:, 2 * hidden :]) * inv * inv / model
        for at, size in tiles(width):
            part = nt(all_ref[:, :hidden], gate_ref[at : at + size, :])
            part = part + nt(all_ref[:, hidden : 2 * hidden], up_ref[at : at + size, :])
            given = inv * gain_ref[:, at : at + size] * part - slot_ref[:, at : at + size].astype(F32) * lean
            given_ref[:, at : at + size] = given.astype(BF)
            put_blocks(given, block_refs, at, size, groups)

    outs = [shape(BF, slots, span), shape(BF, slots, width)] + [fast(BF, groups * CAP, width)] * experts
    res = call(
        kernel, [*map(near, gathered), kept, slot, gain, gate_w, up_w], outs, flops=4 * slots * hidden * width
    )
    return res[0], res[1], res[2:]


def stack(tokens, cotangent, norm_gain, route_gates, expert_ids, expert_map, w_gate, w_up, w_down):
    section = lax.axis_index("section")
    d = lax.axis_index("dp")
    me = lax.axis_index("expert")
    sections, groups, experts = lax.axis_size("section"), lax.axis_size("dp"), lax.axis_size("expert")
    gate_w, up_w, down_w = w_gate[0, 0], w_up[0, 0], w_down[0, 0]
    rows, model = tokens.shape
    width, hidden = gate_w.shape
    own = experts * CAP
    slots = groups * own
    block = groups * CAP
    gain = lax.dynamic_slice(norm_gain, (0, d * width), (1, width))

    matches = expert_ids[0][:, :, None] == expert_map[0][None, None, :]
    chosen = jnp.any(matches, axis=1)
    weight = jnp.sum(jnp.where(matches, route_gates[0][:, :, None], 0.0), axis=1)
    lower = lax.broadcasted_iota(jnp.int32, (rows, rows), 0) > lax.broadcasted_iota(jnp.int32, (rows, rows), 1)
    before = mm(lower.astype(BF), chosen.astype(BF))
    code = jnp.where(chosen, before, -1.0)
    turn = (
        lax.broadcasted_iota(jnp.int32, (experts, experts), 0)
        == (lax.broadcasted_iota(jnp.int32, (experts, experts), 1) + me) % experts
    )
    pick = lambda x: jnp.sum(jnp.where(turn[None], x[:, :, None], 0.0), axis=1)
    mine = jnp.concatenate([pick(code), pick(weight)], axis=1)

    def spread(table, per, count, turned):
        total = table.shape[0]
        col = lax.broadcasted_iota(jnp.int32, (experts, count), 1)
        wide = (col // per == lax.broadcasted_iota(jnp.int32, (experts, count), 0)).astype(BF)
        codes = table[:, :experts].astype(BF)
        weights = split(table[:, experts:])
        slot_col = lax.broadcasted_iota(jnp.int32, (total, count), 1)
        tok_row = lax.broadcasted_iota(jnp.int32, (total, count), 0)
        hit_back = (mm(codes, wide) == (slot_col % CAP).astype(F32)) & (((slot_col // CAP) % (per // CAP) + turned) % (per // CAP) == tok_row // rows)
        slot_row = lax.broadcasted_iota(jnp.int32, (count, total), 0)
        tok_col = lax.broadcasted_iota(jnp.int32, (count, total), 1)
        hit_out = (mm(wide, codes, 0, 1) == (slot_row % CAP).astype(F32)) & (((slot_row // CAP) % (per // CAP) + turned) % (per // CAP) == tok_col // rows)

        def weighted():
            return [jnp.where(hit_back, mm(w, wide), 0.0).astype(BF) for w in weights[:2]]

        def slot_weight():
            full = sum(mm(wide, w, 0, 1) for w in weights)
            return jnp.sum(jnp.where(hit_out, full, 0.0), axis=1, keepdims=True)

        return hit_out, hit_back, weighted, slot_weight

    hit_out, hit_back, own_weighted, own_slot_weight = spread(mine, CAP, own, 0)
    own_out, own_back = hit_out.astype(BF), hit_back.astype(BF)
    own_w = own_weighted()
    own_r = own_slot_weight()

    def after(value, gate):
        return lax.optimization_barrier((value, gate))[0]

    def cut(value, j):
        return lax.dynamic_slice_in_dim(value, ((d + j) % groups) * width, width, axis=1)

    def to_slices(value):
        out = [cut(value, 0)] + [None] * (groups - 1)
        for j in range(1, groups):
            out[groups - j] = ring(cut(value, j), "dp", j)
        return out

    def narrow(value, where):
        out = [cut(value, 0)] + [None] * (groups - 1)
        for j in range(1, groups):
            out[groups - j] = ring_in(cut(value, j), "dp", j, where)
        return out

    def to_rows(parts):
        return [parts[0]] + [ring(parts[j], "dp", j) for j in range(1, groups)]

    def absolute(parts):
        stacked = jnp.stack(parts)
        return jnp.concatenate(
            [lax.dynamic_index_in_dim(stacked, (d - b) % groups, 0, keepdims=False) for b in range(groups)], axis=1
        )

    def by_expert(value):
        shaped = value.reshape(groups, experts, CAP, value.shape[-1])
        return [shaped[:, k].reshape(block, value.shape[-1]) for k in range(experts)]

    def to_experts(blocks, where=None):
        if where is None:
            return [blocks[0]] + [ring(blocks[k], "expert", k) for k in range(1, experts)]
        return [blocks[0]] + [ring_in(blocks[k], "expert", k, where) for k in range(1, experts)]

    def first_cut(value, scale):
        picked = mm(own_out, value)
        if scale is None:
            return to_slices(picked.astype(BF))
        return narrow((scale * picked).astype(BF), (sections - 1,))

    def first_blocks(parts):
        return by_expert(jnp.concatenate(parts, axis=0))

    def reduce_groups(parts):
        return [ring(part, "dp", j + 1) for j, part in enumerate(parts)]

    def gather_groups(value):
        out = [value] + [None] * (groups - 1)
        for j in range(1, groups):
            out[groups - j] = ring(value, "dp", j)
        return out

    def keep(at, latest, earlier):
        if earlier is None:
            return latest
        return jax.tree.map(lambda a, b: jnp.where(section == at, a, b), latest, earlier)

    def own_parts(moved):
        return to_rows([moved[j * own : (j + 1) * own] for j in range(groups)])

    def own_rows(parts):
        whole = absolute(parts)
        blocks = [whole[k * CAP : (k + 1) * CAP] for k in range(experts)]
        return blocks[:1] + send_back(blocks, 1, experts)

    def send_back(blocks, first, last):
        return [ring(blocks[k], "expert", -k) for k in range(first, last)]

    def finish(base, rows_back, tables):
        return (base.astype(F32) + sum(mm(t, rows_back) for t in tables)).astype(BF)

    lower = tuple(range(sections - 1))
    start_parts = first_cut(tokens, None)
    received = to_experts(first_blocks(start_parts))
    codes = after(mine, start_parts)
    codes = [codes] + [ring(codes, "dp", j) for j in range(1, groups)]
    received, codes = lax.optimization_barrier((received, codes))
    here = jnp.concatenate([codes[(groups - j) % groups] for j in range(groups)], axis=0)
    begin = after(tokens, start_parts)
    begin = {j: ring_in(cut(begin, j), "dp", j, lower) for j in (1, 3)}
    hit_out, _, _, here_slot_weight = spread(here, block, slots, 0)
    send_table = hit_out.astype(BF)
    send_r = here_slot_weight()

    saved, back, fills = None, None, {}
    for step in range(sections):
        final_step = step + 1 == sections
        if step:
            state, picked = owner(base, back, behind_w, send_table, None, experts)
            received = to_experts(picked)
        if step and not final_step:
            base = hop(state, 1)
        slot, first, parts = forward_in(received, gain, gate_w, up_w, groups)
        if step == 1:
            fills["early"] = to_experts(first_blocks(after(fills["cut"], parts)))
        parts = reduce_groups(parts)
        payload, gate_pre, up_pre = forward_act(first, parts, model)
        if final_step:
            break
        gathered = gather_groups(payload)
        if step == 1:
            grad0, first0, parts0 = backward_in(after(fills["early"], payload), down_w, groups)
            parts0 = [ring_in(part, "dp", j + 1, (sections - 1,)) for j, part in enumerate(parts0)]
        if step == 0:
            codes = after(here, payload)
            behind, ahead = hop(codes, 1), hop(codes, -1)
            _, _, behind_weighted, _ = spread(behind, block, slots, 0)
            behind_w = behind_weighted()
            _, hit_back, _, _ = spread(ahead, block, slots, 0)
            ahead_t = hit_back.astype(BF)
            far = ring_in(cut(after(tokens, payload), 2), "dp", 2, lower)
            fills["cut"] = first_cut(after(cotangent, payload), own_r)
        kept, out, blocks = forward_out(gathered, down_w, experts)
        back = [hop_back(blocks[k], 1, k) for k in range(experts)]
        if step == 0:
            base = jnp.concatenate([cut(tokens, 0), begin[groups - 1], far, begin[1]], axis=0)
            state = base
        saved = keep(step, (slot, gate_pre, up_pre, kept, out, state), saved)

    at = sections - 1
    slot, gate_pre, up_pre, fwd_state = keep(
        at, (slot, gate_pre, up_pre, state), (saved[0], saved[1], saved[2], saved[5])
    )
    final, base = None, None
    for step in range(sections):
        at = sections - 1 - step
        if step == 0:
            grad = grad0
            payload = backward_act(first0, parts0, gate_pre, up_pre, payload)
            state = jnp.zeros_like(fwd_state)
        else:
            state, picked = owner(base, back, [ahead_t], send_table, send_r, experts)
            received = to_experts(picked)
            if step + 1 < sections:
                base = hop(state, -1)
            else:
                turn_back = jnp.where(section == at, state, final[-1])
                turn_back = [turn_back[j * rows : (j + 1) * rows] for j in range(groups)]
                near_parts = {j: ring_in(turn_back[j], "dp", j, lower) for j in (2, 3)}
            if step == 1:
                received, fills["base"] = lax.optimization_barrier((received, fills["base"]))
            if step == 2:
                received, fills["out"] = lax.optimization_barrier((received, fills["out"]))
            grad, first, parts = backward_in(received, down_w, groups)
            if step == 2:
                whole = absolute(after(fills["out"], parts))
                blocks = [whole[k * CAP : (k + 1) * CAP] for k in range(experts)]
                rows_back = blocks[:1] + send_back(blocks, 1, experts // 2)
            parts = reduce_groups(parts)
            payload = backward_act(first, parts, gate_pre, up_pre)
        gathered = gather_groups(payload)
        if step == 0:
            base = jnp.concatenate(narrow(after(cotangent, payload), lower), axis=0)
            kept, out, _ = forward_out(gathered, down_w, experts)
            kept, fwd_out = keep(at, (kept, out), saved[3:5])
        if step == 2:
            rows_back += send_back(after(blocks, payload), experts // 2, experts)
        grads, given, blocks = backward_out(gathered, kept, slot, gain, gate_w, up_w, experts, model)
        if step + 1 < sections:
            if step == 0:
                held = after(fwd_state, blocks)
                fills["base"] = to_rows([held[j * rows : (j + 1) * rows] for j in range(groups)])
            if step == 1:
                fills["out"] = own_parts(after(fwd_out, blocks))
            back = [hop_back(blocks[k], -1, k) for k in range(experts)]
        final = keep(at, (grad, grads, given, state), final)

    layer_base = jnp.where(section == 0, tokens, absolute(fills["base"]))
    layer_result = finish(layer_base, jnp.concatenate(rows_back, axis=0), own_w)
    grad, grads, given, state = final
    last_parts = own_parts(given)
    last_back = own_rows(last_parts)
    far_part = ring_in(after(turn_back[1], last_parts), "dp", 1, lower)
    last = absolute([turn_back[0], far_part, near_parts[2], near_parts[3]])
    last = jnp.where(section == sections - 1, cotangent, last)
    grad_in = finish(last, jnp.concatenate(last_back, axis=0), [own_back])
    inv_all = from_lanes(kept, hidden)
    normed = (slot.astype(F32) * inv_all * gain).astype(BF)
    down_grad = mm(kept[:, :hidden], grad, 0, 0).astype(BF)
    gate_wgrad = mm(normed, grads[:, :hidden], 0, 0).astype(BF)
    up_wgrad = mm(normed, grads[:, hidden : 2 * hidden], 0, 0).astype(BF)
    return (
        layer_result[None],
        grad_in[None],
        gate_wgrad[None, None],
        up_wgrad[None, None],
        down_grad[None, None],
    )


def solution(mesh):
    return jax.shard_map(
        stack,
        mesh=mesh,
        in_specs=(
            P(("dp", "expert"), None),
            P(("dp", "expert"), None),
            P("section", None),
            P("section", ("dp", "expert"), None),
            P("section", ("dp", "expert"), None),
            P("section", None),
            P("section", "expert", "dp", None),
            P("section", "expert", "dp", None),
            P("section", "expert", None, "dp"),
        ),
        out_specs=(
            P("section", ("dp", "expert"), None),
            P("section", ("dp", "expert"), None),
            P("section", "expert", "dp", None),
            P("section", "expert", "dp", None),
            P("section", "expert", None, "dp"),
        ),
        check_vma=False,
    )
```
